512 devices in a mesh: coil: 32 (over x, y), slab: 16 (over z, core).
Axes of the slice: x: 4, y: 8, z: 8, core: 2. Of those that a mesh axis runs over, the one named last changes fastest.
Arguments:
- adjoint_data: float32 [16, 192, 384], P('slab', 'coil'), may hold values from -80 to 80
- denoised: float32 [16, 192, 384], P('slab', 'coil'), may hold values from -8 to 8, as said below
- sensitivity: float32 [32, 16, 192, 384], P('coil', 'slab'), may hold values from -2 to 2, as said below
- kernel: float32 [16, 384, 384], P(None, 'slab'), may hold values from 0.1 to 2, as said below
- conv_in: bfloat16 [54, 64], replicated, may hold values from -0.875 to 0.875
- conv_mid: bfloat16 [1728, 64], replicated, may hold values from -0.15625 to 0.15625
- conv_out: bfloat16 [1728, 2], replicated, may hold values from -0.15625 to 0.15625
Outputs:
- solution: float32 [16, 192, 384], P('slab', 'coil')
- refined: float32 [16, 192, 384], P('slab', 'coil')
The draws below stay inside these ranges and needn't reach their ends.
Inputs may be any that keep to these rules, and one draw needn't show every extreme that they name: `denoised`: real and imaginary parts of the previous cascade's image. `sensitivity`: real and imaginary parts of the coil maps. Positive kernel values.
All inputs are finite; a program needn't handle non-finite values.
Results may differ from the reference program's by a relative error of at most 0.0023.
Values may be sent and summed in bfloat16 or wider, within the bound.
A program may use at most 64 MiB of HBM per device.

```python
import math
import jax
import jax.numpy as jnp
from jax import lax

N = 192
C = 64
ITERS = 2
GRID = 384
NZ = 16
COILS = 32


def cell_grid():
    depth_pos = ((jnp.arange(NZ, dtype=jnp.float32) + 0.5) / NZ)[:, None, None]
    row_pos = ((jnp.arange(N, dtype=jnp.float32) + 0.5) / N)[None, :, None]
    col_pos = ((jnp.arange(N, dtype=jnp.float32) + 0.5) / N)[None, None, :]
    return (depth_pos, row_pos, col_pos)


def phantom(peak, offset):
    depth_pos, row_pos, col_pos = cell_grid()
    first_dx = row_pos - 0.5 - 0.06 * offset
    first_dy = col_pos - 0.45
    second_dx = row_pos - 0.33
    second_dy = col_pos - 0.62 - 0.05 * offset
    magnitude = peak * jnp.exp(-(first_dx * first_dx + first_dy * first_dy) / 0.08)
    magnitude = magnitude + 0.5 * peak * jnp.exp(-(second_dx * second_dx + second_dy * second_dy) / 0.02)
    magnitude = magnitude * (0.6 + 0.8 * depth_pos)
    phase = 1.1 * row_pos - 0.7 * col_pos + 0.5 * depth_pos + 0.3 * offset
    return jnp.concatenate([magnitude * jnp.cos(phase), magnitude * jnp.sin(phase)], axis=-1)


def draw_adjoint_data(key, part):
    key_base, key_rows, key_cols = jax.random.split(key, 3)
    depth_pos = jnp.arange(NZ, dtype=jnp.float32)[:, None, None] / NZ
    row_pos = jnp.arange(N, dtype=jnp.float32)[None, :, None] / N
    row_scale = jnp.exp(jax.random.uniform(key_rows, (1, N, 1), minval=-1.15, maxval=1.15))
    col_scale = jnp.exp(jax.random.uniform(key_cols, (1, 1, 2 * N), minval=-1.15, maxval=1.15))
    rise_factor = jnp.exp(0.6931 * (row_pos + depth_pos))
    base_values = jnp.clip(jax.random.normal(key_base, (NZ, N, 2 * N)), -4.0, 4.0)
    return 0.3 * rise_factor * row_scale * col_scale * base_values + rise_factor * phantom(1.8, 0.0)


def draw_denoised(key, part):
    noise_part = 0.7 * jnp.clip(jax.random.normal(key, (NZ, N, 2 * N)), -4.0, 4.0)
    return noise_part + phantom(1.2, 1.0)


def draw_sensitivity(key, part):
    key_centre, key_phase, key_rough = jax.random.split(key, 3)
    coil_pos = jnp.arange(COILS, dtype=jnp.float32)[:, None, None, None]
    depth_pos = ((jnp.arange(NZ, dtype=jnp.float32) + 0.5) / NZ)[None, :, None, None]
    row_pos = ((jnp.arange(N, dtype=jnp.float32) + 0.5) / N)[None, None, :, None]
    col_pos = ((jnp.arange(N, dtype=jnp.float32) + 0.5) / N)[None, None, None, :]
    row_centre = (coil_pos + 0.5) / COILS
    col_centre = jax.random.uniform(key_centre, (COILS, 1, 1, 1), minval=0.25, maxval=0.75)
    coil_phase = jax.random.uniform(key_phase, (COILS, 1, 1, 1), minval=-math.pi, maxval=math.pi)
    spread = 2.5 / COILS
    rough = jnp.exp(jax.random.uniform(key_rough, (COILS, NZ, N, N), minval=-0.35, maxval=0.35))
    row_gap = (row_pos - row_centre) / spread
    bump = jnp.exp(-row_gap * row_gap) * (0.6 + 0.4 * jnp.cos(math.pi * (col_pos - col_centre)))
    amplitude = (0.35 + 1.2 * bump) * (0.8 + 0.4 * depth_pos)
    magnitude = 2.0 / math.sqrt(COILS) * amplitude * rough
    phase = coil_phase + 0.9 * row_pos - 0.6 * col_pos + 0.3 * depth_pos
    return jnp.concatenate([magnitude * jnp.cos(phase), magnitude * jnp.sin(phase)], axis=-1)


def draw_kernel(key, part):
    key_radius, key_tilt, key_rough = jax.random.split(key, 3)
    depth_index = jnp.arange(NZ, dtype=jnp.float32)
    depth_freq = (jnp.minimum(depth_index, NZ - depth_index) / (NZ / 2.0))[:, None, None]
    grid_index = jnp.arange(GRID, dtype=jnp.float32)
    grid_freq = jnp.minimum(grid_index, GRID - grid_index) / (GRID / 2.0)
    row_freq = grid_freq[None, :, None]
    col_freq = grid_freq[None, None, :]
    radius = jax.random.uniform(key_radius, (), minval=0.06, maxval=0.12)
    rough = jnp.exp(jax.random.uniform(key_rough, (NZ, GRID, GRID), minval=-0.45, maxval=0.45))
    tilt = jax.random.uniform(key_tilt, (), minval=0.1, maxval=0.5)
    radial = (row_freq * row_freq + col_freq * col_freq) / (radius * radius)
    profile = (0.25 + 1.0 / (1.0 + radial)) * (1.0 - tilt * depth_freq)
    return jnp.clip(profile * rough, 0.1, 2.0)


def gaussian(key, dims, deviation, most, kind=jnp.bfloat16):
    drawn = deviation * jax.random.normal(key, dims, jnp.float32)
    return jnp.clip(drawn, min=-most, max=most).astype(kind)


def setup_inputs(seed: int = 0) -> dict:
    key_list = jax.random.split(jax.random.key(seed), 8)
    adjoint_data = draw_adjoint_data(jax.random.fold_in(key_list[7], 71), 0)
    denoised = draw_denoised(jax.random.fold_in(key_list[7], 71), 0)
    sensitivity = draw_sensitivity(jax.random.fold_in(key_list[7], 71), 0)
    kernel = draw_kernel(jax.random.fold_in(key_list[7], 71), 0)
    conv_in = gaussian(key_list[4], (54, C), 54 ** -0.5, 0.875)
    conv_mid = gaussian(key_list[5], (27 * C, C), (27 * C) ** -0.5, 0.15625)
    conv_out = gaussian(key_list[6], (27 * C, 2), (27 * C) ** -0.5, 0.15625)
    return dict(adjoint_data=adjoint_data, denoised=denoised, sensitivity=sensitivity, kernel=kernel, conv_in=conv_in, conv_mid=conv_mid, conv_out=conv_out)


reg_weight = 0.5


def as_complex(values):
    half_len = values.shape[-1] // 2
    return lax.complex(values[..., :half_len], values[..., half_len:])


def as_real(values):
    return jnp.concatenate([jnp.real(values), jnp.imag(values)], axis=-1)


def normal_image(direction, sensitivity, kernel):
    image_values = as_complex(direction)
    grid_len = kernel.shape[1]
    side_len = image_values.shape[1]

    def one_coil(running, coil_map):
        coil_values = as_complex(coil_map)
        padded = jnp.pad(coil_values * image_values, ((0, 0), (0, grid_len - side_len), (0, grid_len - side_len)))
        spectrum = jnp.fft.fftn(padded, axes=(0, 1, 2)) * kernel
        returned = jnp.fft.ifftn(spectrum, axes=(0, 1, 2))[:, :side_len, :side_len]
        return running + jnp.conj(coil_values) * returned, None

    running, unused = lax.scan(one_coil, jnp.zeros_like(image_values), sensitivity)
    return as_real(running) + reg_weight * direction


def conv_ref(features, weights):
    depth_len = features.shape[0]
    side_len = features.shape[1]
    padded = jnp.pad(features, ((1, 1), (1, 1), (1, 1), (0, 0)))

    def one_plane(plane_index):
        slab_part = lax.dynamic_slice_in_dim(padded, plane_index.astype(jnp.int32), 3, 0)
        tap_list = [slab_part[shift_z, shift_x:shift_x + side_len, shift_y:shift_y + side_len, :]
                    for shift_z in range(3) for shift_x in range(3) for shift_y in range(3)]
        patches = jnp.concatenate(tap_list, axis=-1).reshape(side_len * side_len, -1)
        return jnp.dot(patches, weights, preferred_element_type=jnp.float32).reshape(side_len, side_len, -1)

    return lax.map(one_plane, jnp.arange(depth_len, dtype=jnp.int32))


def reference(adjoint_data, denoised, sensitivity, kernel, conv_in, conv_mid, conv_out):
    right_side = adjoint_data + reg_weight * denoised
    solution = jnp.zeros_like(right_side)
    residual = right_side
    direction = right_side
    norm_now = jnp.sum(residual * residual)
    for iteration in range(ITERS):
        image_out = normal_image(direction, sensitivity, kernel)
        curvature = jnp.sum(direction * image_out)
        step_size = norm_now / curvature
        solution = solution + step_size * direction
        residual = residual - step_size * image_out
        norm_next = jnp.sum(residual * residual)
        direction = residual + (norm_next / norm_now) * direction
        norm_now = norm_next
    side_len = solution.shape[-1] // 2
    channels = jnp.stack([solution[..., :side_len], solution[..., side_len:]], axis=-1).astype(jnp.bfloat16)
    hidden_one = jax.nn.relu(conv_ref(channels, conv_in)).astype(jnp.bfloat16)
    hidden_two = jax.nn.relu(conv_ref(hidden_one, conv_mid)).astype(jnp.bfloat16)
    output_map = conv_ref(hidden_two, conv_out)
    refined = solution + jnp.concatenate([output_map[..., 0], output_map[..., 1]], axis=-1)
    return solution, refined
```

```python
import functools

import jax
import jax.numpy as jnp
import numpy as np
from jax import lax
from jax.experimental import pallas as pl
from jax.experimental.pallas import tpu as pltpu
from jax.sharding import PartitionSpec as P

F32 = jnp.float32
BF16 = jnp.bfloat16
REG = 0.5
ACROSS = 4
TRIM = True


def dft_parts(out_len, in_len, length):
    phases = (np.arange(out_len)[:, None] * np.arange(in_len)[None, :] % length) * (2.0 * np.pi / length)
    return np.cos(phases), np.sin(phases)


def in_bf16(table, parts=1):
    rest, out = table, []
    for _ in range(parts):
        part = rest.astype(np.float32).astype(jnp.bfloat16)
        out.append(part)
        rest = rest - part.astype(np.float64)
    return jnp.asarray(np.stack(out))


def make_tables(slabs, halves, rows, padded, side, grid):
    cos_p, sin_p = dft_parts(grid, side, grid)
    cells = slabs * halves * padded
    keep = np.arange(cells) % padded < rows
    cos_x = np.zeros((grid, cells))
    sin_x = np.zeros((grid, cells))
    cos_x[:, keep] = cos_p
    sin_x[:, keep] = sin_p
    return [
        in_bf16(np.stack([cos_x.T, sin_x.T]), 2),
        in_bf16(np.concatenate([cos_p, sin_p], axis=1), 2),
    ]


def cg_kernel(
    dims,
    adj_ref, den_ref, sens_hbm, kern_hbm, invr_hbm, invl_hbm, cin_hbm, cmid_hbm, cout_hbm,
    both_ref,
    adj_v, den_v, sens_v, kern_v, invr_v, invl_v, cin_v, cmid_v, cout_v,
    depth_t, fwdl_t, fwdr_t, invr_t, invl_t,
    b_own, b_send, b_all, b_far, b_near, b_halo, s_send, s_all, k_all, s_rr, s_ii,
    p_send, p_all, a_send, a_all, c_send, c_all, q_send, q_all, r_send, r_all, d_send, d_all, kf_keep,
    g_send, g_own, r_own_v, r_near, r_halo, n_send, n_sum, n_all, n_tot,
    first_w, mid_w, last_w, taps, taps_t, from_b, from_r, hidden,
    load_sem, send_sem, recv_sem,
):
    coils, slabs, halves, rows, padded, side, grid, feats, total = dims
    width = 2 * side
    cells = slabs * padded * halves
    c = lax.axis_index("coil")
    j = lax.axis_index("slab")
    home = c // halves
    across = ACROSS
    line = coils // across
    my_x = c // line
    my_y = lax.rem(c, line)
    lane = lax.broadcasted_iota(jnp.int32, (cells, width), 1)
    low = lane < side
    row_in_chunk = lax.rem(lax.broadcasted_iota(jnp.int32, (cells, width), 0), padded)
    barrier = pltpu.get_barrier_semaphore()
    native_coil = halves * j + lax.rem(c, halves)
    native_slab = c // halves

    def hello(coil, slab):
        pl.semaphore_signal(barrier, inc=1, device_id=to(coil, slab), device_id_type=pl.DeviceIdType.MESH)

    def to(coil, slab):
        return {"coil": coil, "slab": slab}

    def repeat(first, last, body):
        def step(k, carry):
            body(k)
            return carry

        lax.fori_loop(first, last, step, 0)

    loads = (
        (adj_ref, adj_v), (den_ref, den_v), (sens_hbm.at[0, 0], sens_v), (kern_hbm, kern_v),
        (invl_hbm, invl_v), (invr_hbm, invr_v), (cin_hbm, cin_v), (cmid_hbm, cmid_v), (cout_hbm, cout_v),
    )
    for index, (src, dst) in enumerate(loads):
        pltpu.make_async_copy(src, dst, load_sem.at[index]).start()

    def loaded(index):
        src, dst = loads[index]
        pltpu.make_async_copy(src, dst, load_sem.at[index]).wait()

    repeat(1, slabs, lambda k: hello(c, lax.rem(j + k, slabs)))
    repeat(1, coils, lambda k: hello(lax.rem(c + k, coils), j))

    def trim(ref):
        return ref.at[..., 0:rows, :] if TRIM else ref

    def tidy(values):
        return jnp.where(row_in_chunk < rows, values, 0.0) if TRIM else values

    def swap(values):
        return pltpu.roll(values, side, 1)

    def turn(values):
        rolled = swap(values)
        return jnp.where(low, -rolled, rolled)

    def remote(src, dst, phase, coil, slab):
        return pltpu.make_async_remote_copy(
            src_ref=src,
            dst_ref=dst,
            send_sem=send_sem.at[phase],
            recv_sem=recv_sem.at[phase],
            device_id=to(coil, slab),
            device_id_type=pl.DeviceIdType.MESH,
        )

    def took(ref, phase):
        pltpu.make_async_copy(ref, ref, recv_sem.at[phase]).wait()

    def sent(ref, phase):
        pltpu.make_async_copy(ref, ref, send_sem.at[phase]).wait()

    def to_slabs(src, dst, phase, short=False):
        view = trim if short else lambda ref: ref

        def step(k):
            other = lax.rem(j + k, slabs)
            remote(view(src.at[other]), view(dst.at[j]), phase, c, other).start()

        repeat(1, slabs, step)

    def to_coils(pick, dst, phase):
        def step(k, carry):
            other = lax.rem(c + k, coils)
            remote(pick(other), dst, phase, other, j).start()
            return carry

        lax.fori_loop(1, coils, step, 0)

    def to_beside(src, dst, phase, values=None):
        if values is not None:
            src[...] = values
        remote(src, dst.at[0], phase, lax.rem(c + 1, coils), j).start()
        remote(src, dst.at[1], phase, lax.rem(c + coils - 1, coils), j).start()
        dst[2] = src[...]

    def to_planes(src, dst, phase):
        def step(k):
            remote(src, dst.at[k], phase, c, lax.rem(j + 3 - k + slabs, slabs)).start()

        repeat(0, 3, step)
        repeat(4, 7, step)
        dst[3] = src[...]

    loaded(0)
    loaded(1)
    right = adj_v[:, 0, :] + REG * den_v[:, 0, :]
    b_own[...] = jnp.zeros_like(b_own)
    b_own[0:rows] = right
    b_send[...] = b_own[...].astype(BF16)
    b_all[0] = jnp.zeros_like(b_send)
    b_all[coils + 1] = jnp.zeros_like(b_send)
    b_all[c + 1] = b_send[...]

    pl.semaphore_wait(barrier, (slabs - 1) + (coils - 1))

    to_coils(lambda other: trim(b_send), trim(b_all.at[c + 1]), 0)
    to_beside(b_own, b_near, 16)

    far_row = j // across
    near_row = lax.rem(j, across)
    mine = near_row == my_x
    loaded(3)

    @pl.when(mine)
    def _():
        def share(k):
            other = lax.rem(j + k, slabs)
            remote(kern_v.at[other], k_all.at[far_row, near_row], 2, c, other).start()

        repeat(1, slabs, share)
        k_all[far_row, near_row] = kern_v[j]

    loaded(2)
    for block in range(slabs):
        for half in range(halves):
            first = (block * halves + half) * rows
            piece = sens_v[first : first + rows, :]
            piece = jnp.concatenate([piece, jnp.zeros((padded - rows, width), F32)], axis=0)
            s_send[block, half] = piece.astype(BF16)
            s_rr[first // rows * padded : (first // rows + 1) * padded] = piece
    to_slabs(s_send, s_all, 1, True)
    s_all[j] = s_send[j]
    maps = s_rr[...]
    rolled = swap(maps)
    s_rr[...] = jnp.where(low, maps, rolled)
    s_ii[...] = jnp.where(low, -rolled, maps)

    square = slabs * halves * padded
    row = lax.broadcasted_iota(jnp.int32, (square, square), 0)
    col = lax.broadcasted_iota(jnp.int32, (square, square), 1)
    group = halves * padded
    turns = lax.rem((row // group) * (col // group), slabs)
    same = (lax.rem(row, group) == lax.rem(col, group)) & (lax.rem(row, padded) < rows)
    turns = jnp.where(same, turns, slabs)
    for part, values in enumerate(dft_parts(slabs, 2, slabs)):
        table = jnp.zeros((square, square), F32)
        for index in range(slabs):
            table = jnp.where(turns == index, float(values[index, 1]), table)
        high = table.astype(BF16)
        depth_t[0, part * square : (part + 1) * square] = high
        depth_t[1, part * square : (part + 1) * square] = (table - high.astype(F32)).astype(BF16)
    loaded(4)
    for part in range(2):
        top = invl_v[part].astype(F32)
        turned = pltpu.roll(top, side, 1)
        left = lax.broadcasted_iota(jnp.int32, top.shape, 1) < side
        invl_t[part, 0:grid] = invl_v[part]
        invl_t[part, grid:] = jnp.where(left, -turned, turned).astype(BF16)
    flipped = jnp.transpose(invl_v[0].astype(F32)).astype(BF16)
    fwdl_t[:, 0:grid] = flipped
    fwdl_t[0:side, grid:] = -flipped[side:]
    fwdl_t[side:, grid:] = flipped[:side]
    loaded(5)
    cosines = jnp.transpose(invr_v[0, 0].astype(F32)).astype(BF16)
    sines = jnp.transpose(invr_v[0, 1].astype(F32)).astype(BF16)
    fwdr_t[0:grid, 0:cells] = cosines
    fwdr_t[0:grid, cells:] = sines
    fwdr_t[grid:, 0:cells] = -sines
    fwdr_t[grid:, cells:] = cosines
    for part in range(2):
        invr_t[part, 0:cells, 0:grid] = invr_v[part, 0]
        invr_t[part, 0:cells, grid:] = -invr_v[part, 1]
        invr_t[part, cells:, 0:grid] = invr_v[part, 1]
        invr_t[part, cells:, grid:] = invr_v[part, 0]

    def depth_dft(image):
        both = jnp.dot(depth_t[0], image, preferred_element_type=F32)
        both = both + jnp.dot(depth_t[1], image, preferred_element_type=F32)
        return both[:cells], turn(both[cells:])

    def coil_images(field):
        field = tidy(field)
        product = s_rr[...] * field + s_ii[...] * swap(field)
        return product.astype(BF16)

    def to_depth(product):
        real, imag = depth_dft(product)
        return (real - imag).astype(BF16).reshape(slabs, halves, padded, width)

    def spectrum(image_ref):
        image = tidy(image_ref[...].astype(F32).reshape(cells, width)).astype(BF16)
        lines = jnp.dot(image, fwdl_t[...], preferred_element_type=F32).astype(BF16)
        stacked = jnp.concatenate([lines[:, :grid], lines[:, grid:]], axis=0)
        return jnp.dot(fwdr_t[...], stacked, preferred_element_type=F32)

    took(trim(b_all.at[0 : coils - 1]), 0)
    product = coil_images(b_all[1 : coils + 1].astype(F32).reshape(cells, width))
    p_send[...] = product.astype(F32).reshape(slabs, halves, padded, width).astype(BF16)
    to_slabs(p_send, p_all, 13, True)
    p_all[j] = p_send[j]
    prior_weights(dims, loaded, cin_v, cmid_v, cout_v, first_w, mid_w, last_w)

    half_here = lax.rem(c, halves)

    @pl.when(j == home)
    def _():
        def share(k):
            other = lax.rem(j + k, slabs)
            remote(b_all.at[1 + halves * other + half_here], b_far, 5, c, other).start()

        repeat(1, slabs, share)
        b_far[...] = b_all[1 + halves * j + half_here]

    @pl.when(mine)
    def _():
        took(k_all.at[0, 0 : across - 1], 2)

    @pl.when(jnp.logical_not(mine))
    def _():
        took(k_all.at[0], 2)

    def pass_on(k):
        other = lax.rem(my_x + k, across)
        remote(k_all.at[:, my_x], k_all.at[:, my_x], 15, other * line + my_y, j).start()

    repeat(1, across, pass_on)

    took(trim(p_all.at[0 : slabs - 1]), 13)
    a_send[...] = to_depth(tidy(p_all[...].astype(F32).reshape(cells, width)).astype(BF16))
    to_slabs(a_send, a_all, 4, True)
    a_all[j] = a_send[j]
    took(trim(s_all.at[0 : slabs - 1]), 1)
    maps = tidy(s_all[...].astype(F32).reshape(cells, width))
    rolled = swap(maps)
    s_rr[...] = jnp.where(low, maps, rolled)
    s_ii[...] = jnp.where(low, -rolled, maps)
    took(trim(a_all.at[0 : slabs - 1]), 4)
    took(k_all.at[:, 0 : across - 1], 15)
    weight = k_all[...].reshape(grid, grid)
    freq = spectrum(a_all)
    kf_keep[0:grid] = weight * freq[:grid]
    kf_keep[grid:] = weight * freq[grid:]
    energy = jnp.sum(kf_keep[...] * freq)

    sub = lax.broadcasted_iota(jnp.int32, (8, 128), 0)

    def message(values):
        packed = jnp.zeros((8, 128), F32)
        for index, value in enumerate(values):
            packed = jnp.where(sub == index, value, packed)
        return packed

    third = lax.broadcasted_iota(jnp.int32, (1, width), 1) // (width // 3)

    def as_parts(value):
        value = jnp.broadcast_to(value, (1, width))
        high = value.astype(BF16).astype(F32)
        mid = (value - high).astype(BF16).astype(F32)
        return jnp.where(third == 0, high, jnp.where(third == 1, mid, value - high - mid))

    def with_sums(values, first_sum, second_sum):
        values = jnp.where(row_in_chunk == rows, as_parts(first_sum), values)
        return jnp.where(row_in_chunk == rows + 1, as_parts(second_sum), values)

    def from_parts(line):
        size = width // 3
        joined = line[:, 0:size] + line[:, size : 2 * size] + line[:, 2 * size :]
        return joined[:, 0:1]

    def sum_slabs(src, dst, phase):
        def step(k, carry):
            other = lax.rem(j + k, slabs)
            remote(src, dst.at[j], phase, c, other).start()
            return carry

        lax.fori_loop(1, slabs, step, 0)
        dst[j] = src[...]

    scaled = kf_keep[...].astype(BF16)
    back = jnp.dot(invr_t[0], scaled, preferred_element_type=F32)
    back = (back + jnp.dot(invr_t[1], scaled, preferred_element_type=F32)).astype(BF16)
    back = jnp.concatenate([back[:cells], back[cells:]], axis=1)
    image = jnp.dot(back, invl_t[0], preferred_element_type=F32)
    image = (image + jnp.dot(back, invl_t[1], preferred_element_type=F32)) * (1.0 / total)
    bb_part = jnp.sum(right * right)
    image = with_sums(image, energy * (1.0 / total), bb_part)
    c_send[...] = image.astype(BF16).reshape(slabs, halves, padded, width)
    to_slabs(c_send, c_all, 6)
    c_all[j] = c_send[j]
    took(c_all.at[0 : slabs - 1], 6)
    sums = jnp.sum(c_all[:, 0].astype(F32), axis=0)
    energy_sum = from_parts(sums[rows : rows + 1])
    bb_sum = from_parts(sums[rows + 1 : rows + 2])
    image = c_all[...].astype(F32).reshape(cells, width)
    image = jnp.where(row_in_chunk < rows, image, 0.0).astype(BF16)
    real, imag = depth_dft(image)
    image = real + imag
    coil_part = s_rr[...] * image - s_ii[...] * swap(image)
    q_send[...] = with_sums(coil_part, energy_sum, bb_sum).astype(BF16).reshape(coils, padded, width)
    to_coils(lambda other: q_send.at[other], q_all.at[c], 8)
    q_all[c] = q_send[c]

    took(b_near.at[0:2], 16)
    to_planes(b_near, b_halo, 3)

    @pl.when(j != home)
    def _():
        took(b_far, 5)

    chunk_row = lax.broadcasted_iota(jnp.int32, (padded, width), 0)
    b_here = jnp.where(chunk_row < rows, b_far[...].astype(F32), 0.0)
    took(q_all.at[0 : coils - 1], 8)
    sums = jnp.sum(q_all[...].astype(F32), axis=0)
    g_coils = jnp.where(chunk_row < rows, sums, 0.0)
    g_send[...] = g_coils
    g_here = g_coils + REG * b_here
    energy0 = from_parts(sums[rows : rows + 1])
    bb = from_parts(sums[rows + 1 : rows + 2])
    alpha0 = bb / (energy0 + REG * bb)
    resid = b_here - alpha0 * g_here
    r_send[...] = resid.astype(BF16)
    to_coils(lambda other: trim(r_send), trim(r_all.at[c]), 9)
    r_all[c] = r_send[...]

    @pl.when(j == home)
    def _():
        pltpu.make_async_copy(g_send, g_own, recv_sem.at[10]).start()

    @pl.when(j != home)
    def _():
        remote(g_send, g_own, 10, native_coil, native_slab).start()

    rr_part = jnp.sum(resid * resid)
    rb_part = jnp.sum(resid * b_here)

    took(b_halo.at[0:6], 3)
    prior_taps(dims, c, j, b_halo[...], taps, taps_t)
    prior_sums(dims, 0, taps_t, first_w, from_b)

    took(trim(r_all.at[0 : coils - 1]), 9)
    d_send[...] = to_depth(coil_images(r_all[...].astype(F32).reshape(cells, width)))
    to_slabs(d_send, d_all, 11, True)
    d_all[j] = d_send[j]
    took(g_own, 10)
    r_own = b_own[...] - alpha0 * (g_own[...] + REG * b_own[...])
    to_beside(r_own_v, r_near, 17, r_own)
    prior_sums(dims, 1, taps_t, first_w, from_b)
    took(r_near.at[0:2], 17)
    to_planes(r_near, r_halo, 12)

    took(trim(d_all.at[0 : slabs - 1]), 11)
    freq = spectrum(d_all)
    cross = jnp.sum(kf_keep[...] * freq)
    power = freq * freq
    energy = jnp.sum(weight * (power[:grid] + power[grid:]))
    n_send[...] = message([energy * (1.0 / total), cross * (1.0 / total), rr_part, rb_part])
    sum_slabs(n_send, n_all, 7)
    took(r_halo.at[0:6], 12)
    prior_taps(dims, c, j, r_halo[...], taps, taps_t)
    prior_sums(dims, 0, taps_t, first_w, from_r)
    took(n_all.at[0 : slabs - 1], 7)
    n_sum[...] = jnp.sum(n_all[...], axis=0)
    to_coils(lambda other: n_sum, n_tot.at[c], 14)
    n_tot[c] = n_sum[...]
    prior_sums(dims, 1, taps_t, first_w, from_r)

    took(n_tot.at[0 : coils - 1], 14)
    sums = jnp.sum(n_tot[...], axis=0)
    energy1 = sums[0:1, 0:1]
    cross1 = sums[1:2, 0:1]
    rr = sums[2:3, 0:1]
    rb = sums[3:4, 0:1]
    beta = rr / bb
    curvature = energy1 + 2.0 * beta * cross1 + beta * beta * energy0
    curvature = curvature + REG * (rr + 2.0 * beta * rb + beta * beta * bb)
    alpha1 = rr / curvature
    for_b = alpha0 + alpha1 * beta
    solved = (for_b * b_own[...] + alpha1 * r_own)[0:rows]
    for r in range(rows):
        both_ref[r] = solved[r : r + 1]
    prior_rest(dims, c, j, for_b, alpha1, from_b, from_r, hidden, mid_w, last_w, solved, both_ref.at[pl.ds(rows, rows)])

    @pl.when(j != home)
    def _():
        sent(g_send, 10)

    @pl.when(j == home)
    def _():
        sent(b_all.at[0 : slabs - 1], 5)

    @pl.when(mine)
    def _():
        sent(kern_v.at[0 : slabs - 1], 2)

    sent(trim(b_all.at[0 : coils - 1]), 0)
    sent(trim(s_all.at[0 : slabs - 1]), 1)
    sent(b_halo.at[0:6], 3)
    sent(b_near.at[0:2], 16)
    sent(trim(a_all.at[0 : slabs - 1]), 4)
    sent(c_all.at[0 : slabs - 1], 6)
    sent(n_all.at[0 : slabs - 1], 7)
    sent(q_all.at[0 : coils - 1], 8)
    sent(trim(r_all.at[0 : coils - 1]), 9)
    sent(trim(d_all.at[0 : slabs - 1]), 11)
    sent(r_halo.at[0:6], 12)
    sent(r_near.at[0:2], 17)
    sent(trim(p_all.at[0 : slabs - 1]), 13)
    sent(n_tot.at[0 : coils - 1], 14)
    sent(k_all.at[:, 0 : across - 1], 15)


def prior_weights(dims, loaded, cin_v, cmid_v, cout_v, first_w, mid_w, last_w):
    coils, slabs, halves, rows, padded, side, grid, feats, total = dims
    strip = 3 * padded
    deep = rows + 4
    loaded(6)
    tap_shape = (54, 18 * strip)
    tap = lax.broadcasted_iota(jnp.int32, tap_shape, 0)
    at = lax.broadcasted_iota(jnp.int32, tap_shape, 1)
    kind = at // strip
    place = lax.rem(at, strip)
    inner = lax.rem(place, padded)
    image_row = (place // padded) * rows + inner
    rest = tap - (kind // 6) * 18 - lax.rem(kind, 6)
    for r in range(deep):
        dx = image_row - (r + 3)
        hit = (rest == dx * 6) & (dx >= 0) & (dx < 3) & (inner < rows)
        pick = jnp.where(hit, 1.0, 0.0).astype(BF16)
        part = lax.dot_general(cin_v[...], pick, (((0,), (0,)), ((), ())), preferred_element_type=F32).astype(BF16)
        first_w[2 * r * feats : (2 * r + 1) * feats] = part
        if r > 0:
            first_w[(2 * r - 1) * feats : 2 * r * feats] = part
    first_w[(2 * deep - 1) * feats :] = jnp.zeros((feats, 18 * strip), BF16)
    loaded(7)
    mid_w[...] = jnp.zeros_like(mid_w)
    loaded(8)
    last_w[...] = jnp.zeros_like(last_w)
    for dz in range(3):
        for dx in range(3):
            for dy in range(3):
                first = ((dz * 3 + dx) * 3 + dy) * feats
                block = cmid_v[:, first : first + feats]
                for place in ((0,), (2, 3), (1,))[dy]:
                    mid_w[dz, place * feats : (place + 1) * feats, dx * feats : (dx + 1) * feats] = block
                last_w[dz, dy * 2 : dy * 2 + 2, dx * feats : (dx + 1) * feats] = cout_v[:, first : first + feats]


def shift_lanes(values, up):
    at = lax.broadcasted_iota(jnp.int32, values.shape, 1)
    count = values.shape[1]
    if up:
        return jnp.where(at == 0, 0.0, pltpu.roll(values, 1, 1))
    return jnp.where(at == count - 1, 0.0, pltpu.roll(values, count - 1, 1))


def prior_taps(dims, c, j, field, taps, taps_t):
    coils, slabs, halves, rows, padded, side, grid, feats, total = dims
    strip = 3 * padded
    width = 2 * side
    field = jnp.stack([field[:, k] for k in (0, 2, 1)], axis=1).reshape(21, padded, width)
    index = lax.broadcasted_iota(jnp.int32, (21, padded, width), 0)
    plane = j + index // 3 - 3
    chunk = c + lax.rem(index, 3) - 1
    inside = (plane >= 0) & (plane < slabs) & (chunk >= 0) & (chunk < coils)
    inside = inside & (lax.broadcasted_iota(jnp.int32, (21, padded, width), 1) < rows)
    field = jnp.where(inside, field, 0.0).reshape(7 * strip, width)
    for part in range(2):
        values = field[:, part * side : (part + 1) * side]
        for dy, shifted in enumerate((shift_lanes(values, True), values, shift_lanes(values, False))):
            taps[:, dy * 2 + part] = shifted.reshape(7, strip, side)
    for p in range(5):
        part = jnp.transpose(taps[p : p + 3].reshape(3 * 6 * strip, side))
        high = part.astype(BF16)
        taps_t[0, p] = high
        taps_t[1, p] = (part - high.astype(F32)).astype(BF16)


def prior_sums(dims, turn, taps_t, first_w, result):
    coils, slabs, halves, rows, padded, side, grid, feats, total = dims
    first, last = ((0, 2), (2, 5))[turn]
    inner = 18 * 3 * padded
    contract = (((1,), (1,)), ((), ()))
    tall = (last - first) * side
    high = taps_t[0, first:last].reshape(tall, inner)
    low = taps_t[1, first:last].reshape(tall, inner)
    sums = lax.dot_general(high, first_w[...], contract, preferred_element_type=F32)
    sums = sums + lax.dot_general(low, first_w[...], contract, preferred_element_type=F32)
    result[first:last] = sums.reshape(last - first, side, sums.shape[1])


def prior_rest(dims, c, j, for_b, for_r, from_b, from_r, hidden, mid_w, last_w, solved, out_ref):
    coils, slabs, halves, rows, padded, side, grid, feats, total = dims
    width = 2 * side
    pair = 2 * feats
    deep = rows + 4
    deep_lane = lax.broadcasted_iota(jnp.int32, (1, deep * pair), 1)
    out_row = deep_lane // pair + lax.rem(deep_lane, pair) // feats
    at_row = c * rows - 2 + out_row
    row_ok = (at_row >= 0) & (at_row < side) & (out_row < deep)
    for p in range(5):
        at_plane = j + p - 2
        ok = row_ok & (at_plane >= 0) & (at_plane < slabs)
        scale_b = jnp.where(ok, for_b, 0.0)
        scale_r = jnp.where(ok, for_r, 0.0)
        for r in range(deep):
            span = slice(r * pair, (r + 1) * pair)
            feat = from_b[p, :, span] * scale_b[:, span] + from_r[p, :, span] * scale_r[:, span]
            hidden[p, r] = jnp.maximum(feat, 0.0).astype(BF16)
    wide = rows + 2
    cell = lax.broadcasted_iota(jnp.int32, (side, pair), 0)
    left = lax.broadcasted_iota(jnp.int32, (side, pair), 1) < feats
    result = None
    for p in range(3):
        feat = None
        for dz in range(3):
            data = jnp.concatenate(
                [
                    hidden[p + dz, 0:wide].reshape(wide * side, pair),
                    hidden[p + dz, 2 : wide + 2].reshape(wide * side, pair),
                ],
                axis=1,
            )
            piece = lax.dot_general(data, mid_w[dz], (((1,), (1,)), ((), ())), preferred_element_type=F32)
            feat = piece if feat is None else feat + piece
        at_plane = j + p - 1
        plane_ok = (at_plane >= 0) & (at_plane < slabs)
        maps = []
        for r in range(wide):
            sides = feat[r * side : (r + 1) * side, :pair]
            centre = feat[r * side : (r + 1) * side, pair:]
            ahead = jnp.where(cell == 0, 0.0, pltpu.roll(sides, 1, 0))
            behind = jnp.where(cell == side - 1, 0.0, pltpu.roll(sides, side - 1, 0))
            sides = jnp.where(left, ahead, behind)
            value = jnp.maximum(sides + pltpu.roll(sides, feats, 1) + centre, 0.0)
            at_row = c * rows - 1 + r
            ok = plane_ok & (at_row >= 0) & (at_row < side)
            maps.append(jnp.where(ok, value, 0.0).astype(BF16))
        pairs = [jnp.where(left, maps[r], maps[r + 1]) for r in range(wide - 1)]
        pairs.append(maps[wide - 1])
        data = jnp.concatenate(
            [jnp.concatenate(pairs[0:rows], axis=0), jnp.concatenate(pairs[2 : rows + 2], axis=0)], axis=1
        )
        piece = lax.dot_general(last_w[p], data, (((1,), (1,)), ((), ())), preferred_element_type=F32)
        result = piece if result is None else result + piece
    for r in range(rows):
        span = result[:, r * side : (r + 1) * side]
        value = shift_lanes(span, True)[0:2] + span[2:4] + shift_lanes(span, False)[4:6]
        out_ref[r, :, 0:side] = solved[r : r + 1, 0:side] + value[0:1]
        out_ref[r, :, side:width] = solved[r : r + 1, side:width] + value[1:2]


def shards(adjoint_data, denoised, sensitivity, kernel, conv_in, conv_mid, conv_out):
    coils = lax.axis_size("coil")
    slabs = lax.axis_size("slab")
    rows = adjoint_data.shape[1]
    width = adjoint_data.shape[2]
    side = sensitivity.shape[2]
    grid = kernel.shape[2]
    feats = conv_mid.shape[1]
    halves = coils // slabs
    padded = 8
    deep = rows + 4
    total = float(slabs * grid * grid)
    dims = (coils, slabs, halves, rows, padded, side, grid, feats, total)
    tables = make_tables(slabs, halves, rows, padded, side, grid)
    cells = slabs * halves * padded
    kx = kernel.shape[1]
    layers = (conv_in, conv_mid.T, conv_out.T)
    vmem = pltpu.VMEM
    block = (slabs, halves, padded, width)
    strip = 3 * padded
    scratch = [
        vmem((rows, 1, width), F32), vmem((rows, 1, width), F32), vmem((side, width), F32), vmem((slabs, kx, grid), F32),
        *[vmem(t.shape, BF16) for t in (*tables, *layers)],
        vmem((2, 2 * cells, cells), BF16), vmem((2 * side, 2 * grid), BF16), vmem((2 * grid, 2 * cells), BF16),
        vmem((2, 2 * cells, 2 * grid), BF16), vmem((2, 2 * grid, 2 * side), BF16),
        vmem((padded, width), F32), vmem((padded, width), BF16), vmem((coils + 2, padded, width), BF16),
        vmem((padded, width), BF16), vmem((3, padded, width), F32), vmem((7, 3, padded, width), F32),
        vmem(block, BF16), vmem(block, BF16),
        vmem((slabs // ACROSS, ACROSS, kx, grid), F32),
        vmem((cells, width), F32), vmem((cells, width), F32),
        *[vmem(block, BF16)] * 6,
        vmem((coils, padded, width), BF16), vmem((coils, padded, width), BF16),
        vmem((padded, width), BF16), vmem((coils, padded, width), BF16),
        vmem(block, BF16), vmem(block, BF16),
        vmem((2 * grid, grid), F32),
        vmem((padded, width), F32), vmem((padded, width), F32),
        vmem((padded, width), F32), vmem((3, padded, width), F32), vmem((7, 3, padded, width), F32),
        vmem((8, 128), F32), vmem((8, 128), F32), vmem((slabs, 8, 128), F32), vmem((coils, 8, 128), F32),
        vmem((2 * deep * feats, 18 * strip), BF16), vmem((3, 4 * feats, 4 * feats), BF16), vmem((3, 8, 4 * feats), BF16),
        vmem((7, 6, strip, side), F32), vmem((2, 5, side, 18 * strip), BF16),
        vmem((5, side, 2 * deep * feats), F32), vmem((5, side, 2 * deep * feats), F32),
        vmem((5, deep, side, 2 * feats), BF16),
        pltpu.SemaphoreType.DMA((9,)), pltpu.SemaphoreType.DMA((18,)), pltpu.SemaphoreType.DMA((18,)),
    ]
    near = pl.BlockSpec(memory_space=pltpu.VMEM)
    far = pl.BlockSpec(memory_space=pltpu.HBM)
    shape = jax.ShapeDtypeStruct((2 * rows, 1, width), F32)
    both = pl.pallas_call(
        functools.partial(cg_kernel, dims),
        out_shape=shape,
        in_specs=[far] * 9,
        out_specs=near,
        scratch_shapes=scratch,
        compiler_params=pltpu.CompilerParams(has_side_effects=True, collective_id=0, vmem_limit_bytes=60 << 20),
        name="cg",
    )(adjoint_data.transpose(1, 0, 2), denoised.transpose(1, 0, 2), sensitivity, kernel, *tables, *layers)
    return (both[:rows].transpose(1, 0, 2), both[rows:].transpose(1, 0, 2))


def solution(mesh):
    placed = (
        P("slab", "coil", None),
        P("slab", "coil", None),
        P("coil", "slab", None, None),
        P(None, "slab", None),
        P(),
        P(),
        P(),
    )
    return jax.shard_map(
        shards,
        mesh=mesh,
        in_specs=placed,
        out_specs=(P("slab", "coil", None), P("slab", "coil", None)),
        check_vma=False,
    )
```

```python
import functools

import jax
import jax.numpy as jnp
import numpy as np
from jax import lax
from jax.experimental import pallas as pl
from jax.experimental.pallas import tpu as pltpu
from jax.sharding import PartitionSpec as P

F32 = jnp.float32
BF16 = jnp.bfloat16
REG = 0.5
ACROSS = 4
TRIM = True


def dft_parts(out_len, in_len, length):
    phases = (np.arange(out_len)[:, None] * np.arange(in_len)[None, :] % length) * (2.0 * np.pi / length)
    return np.cos(phases), np.sin(phases)


def in_bf16(table, parts=1):
    rest, out = table, []
    for _ in range(parts):
        part = rest.astype(np.float32).astype(jnp.bfloat16)
        out.append(part)
        rest = rest - part.astype(np.float64)
    return jnp.asarray(np.stack(out))


def make_tables(slabs, halves, rows, padded, side, grid):
    cos_p, sin_p = dft_parts(grid, side, grid)
    cells = slabs * halves * padded
    keep = np.arange(cells) % padded < rows
    cos_x = np.zeros((grid, cells))
    sin_x = np.zeros((grid, cells))
    cos_x[:, keep] = cos_p
    sin_x[:, keep] = sin_p
    return [
        in_bf16(np.stack([cos_x.T, sin_x.T]), 2),
        in_bf16(np.concatenate([cos_p, sin_p], axis=1), 2),
    ]


def cg_kernel(
    dims,
    adj_ref, den_ref, sens_hbm, kern_hbm, invr_hbm, invl_hbm, cin_hbm, cmid_hbm, cout_hbm,
    both_ref,
    adj_v, den_v, sens_v, kern_v, invr_v, invl_v, cin_v, cmid_v, cout_v,
    depth_t, fwdl_t, fwdr_t, invr_t, invl_t,
    b_own, b_send, b_all, b_far, b_near, b_halo, s_send, s_all, k_all, s_rr, s_ii,
    p_send, p_all, a_send, a_all, c_send, c_all, q_send, q_all, r_send, r_all, d_send, d_all, kf_keep,
    g_send, g_own, r_own_v, r_near, r_halo, n_send, n_sum, n_all, n_tot,
    first_w, mid_w, last_w, taps, taps_t, from_b, from_r, hidden,
    load_sem, send_sem, recv_sem,
):
    coils, slabs, halves, rows, padded, side, grid, feats, total = dims
    width = 2 * side
    cells = slabs * padded * halves
    c = lax.axis_index("coil")
    j = lax.axis_index("slab")
    home = c // halves
    across = ACROSS
    line = coils // across
    my_x = c // line
    my_y = lax.rem(c, line)
    lane = lax.broadcasted_iota(jnp.int32, (cells, width), 1)
    low = lane < side
    row_in_chunk = lax.rem(lax.broadcasted_iota(jnp.int32, (cells, width), 0), padded)
    barrier = pltpu.get_barrier_semaphore()
    native_coil = halves * j + lax.rem(c, halves)
    native_slab = c // halves

    def hello(coil, slab):
        pl.semaphore_signal(barrier, inc=1, device_id=to(coil, slab), device_id_type=pl.DeviceIdType.MESH)

    def to(coil, slab):
        return {"coil": coil, "slab": slab}

    def repeat(first, last, body):
        def step(k, carry):
            body(k)
            return carry

        lax.fori_loop(first, last, step, 0)

    def far_first(index, count):
        step = (index + 1) // 2
        return count // 2 + step - 2 * step * lax.rem(index, 2)

    def slab_at(index):
        return lax.rem(j + far_first(index, slabs), slabs)

    def coil_at(index):
        along = lax.rem(my_y + far_first(index // across, line), line)
        return lax.rem(my_x + far_first(lax.rem(index, across), across), across) * line + along

    loads = (
        (adj_ref, adj_v), (den_ref, den_v), (sens_hbm.at[0, 0], sens_v), (kern_hbm, kern_v),
        (invl_hbm, invl_v), (invr_hbm, invr_v), (cin_hbm, cin_v), (cmid_hbm, cmid_v), (cout_hbm, cout_v),
    )
    for index, (src, dst) in enumerate(loads):
        pltpu.make_async_copy(src, dst, load_sem.at[index]).start()

    def loaded(index):
        src, dst = loads[index]
        pltpu.make_async_copy(src, dst, load_sem.at[index]).wait()

    repeat(0, coils - 1, lambda k: hello(coil_at(k), j))
    repeat(0, slabs - 1, lambda k: hello(c, slab_at(k)))

    def trim(ref):
        return ref.at[..., 0:rows, :] if TRIM else ref

    def tidy(values):
        return jnp.where(row_in_chunk < rows, values, 0.0) if TRIM else values

    def swap(values):
        return pltpu.roll(values, side, 1)

    def turn(values):
        rolled = swap(values)
        return jnp.where(low, -rolled, rolled)

    def remote(src, dst, phase, coil, slab):
        return pltpu.make_async_remote_copy(
            src_ref=src,
            dst_ref=dst,
            send_sem=send_sem.at[phase],
            recv_sem=recv_sem.at[phase],
            device_id=to(coil, slab),
            device_id_type=pl.DeviceIdType.MESH,
        )

    def took(ref, phase):
        pltpu.make_async_copy(ref, ref, recv_sem.at[phase]).wait()

    def sent(ref, phase):
        pltpu.make_async_copy(ref, ref, send_sem.at[phase]).wait()

    def to_slabs(src, dst, phase, short=False):
        view = trim if short else lambda ref: ref

        def step(k):
            other = slab_at(k)
            remote(view(src.at[other]), view(dst.at[j]), phase, c, other).start()

        repeat(0, slabs - 1, step)

    def to_coils(pick, dst, phase):
        def step(k):
            other = coil_at(k)
            remote(pick(other), dst, phase, other, j).start()

        repeat(0, coils - 1, step)

    def to_beside(src, dst, phase, values=None):
        if values is not None:
            src[...] = values
        remote(src, dst.at[0], phase, lax.rem(c + 1, coils), j).start()
        remote(src, dst.at[1], phase, lax.rem(c + coils - 1, coils), j).start()
        dst[2] = src[...]

    def to_planes(src, dst, phase):
        def step(k):
            remote(src, dst.at[k], phase, c, lax.rem(j + 3 - k + slabs, slabs)).start()

        repeat(0, 3, step)
        repeat(4, 7, step)
        dst[3] = src[...]

    loaded(0)
    loaded(1)
    right = adj_v[:, 0, :] + REG * den_v[:, 0, :]
    b_own[...] = jnp.zeros_like(b_own)
    b_own[0:rows] = right
    b_send[...] = b_own[...].astype(BF16)
    b_all[0] = jnp.zeros_like(b_send)
    b_all[coils + 1] = jnp.zeros_like(b_send)
    b_all[c + 1] = b_send[...]

    pl.semaphore_wait(barrier, (slabs - 1) + (coils - 1))

    to_coils(lambda other: trim(b_send), trim(b_all.at[c + 1]), 0)
    to_beside(b_own, b_near, 16)

    far_row = j // across
    near_row = lax.rem(j, across)
    mine = near_row == my_x
    loaded(3)

    @pl.when(mine)
    def _():
        def share(k):
            other = lax.rem(j + k, slabs)
            remote(kern_v.at[other], k_all.at[far_row, near_row], 2, c, other).start()

        repeat(1, slabs, share)
        k_all[far_row, near_row] = kern_v[j]

    loaded(2)
    for block in range(slabs):
        for half in range(halves):
            first = (block * halves + half) * rows
            piece = sens_v[first : first + rows, :]
            piece = jnp.concatenate([piece, jnp.zeros((padded - rows, width), F32)], axis=0)
            s_send[block, half] = piece.astype(BF16)
            s_rr[first // rows * padded : (first // rows + 1) * padded] = piece
    to_slabs(s_send, s_all, 1, True)
    s_all[j] = s_send[j]
    maps = s_rr[...]
    rolled = swap(maps)
    s_rr[...] = jnp.where(low, maps, rolled)
    s_ii[...] = jnp.where(low, -rolled, maps)

    square = slabs * halves * padded
    row = lax.broadcasted_iota(jnp.int32, (square, square), 0)
    col = lax.broadcasted_iota(jnp.int32, (square, square), 1)
    group = halves * padded
    turns = lax.rem((row // group) * (col // group), slabs)
    same = (lax.rem(row, group) == lax.rem(col, group)) & (lax.rem(row, padded) < rows)
    turns = jnp.where(same, turns, slabs)
    for part, values in enumerate(dft_parts(slabs, 2, slabs)):
        table = jnp.zeros((square, square), F32)
        for index in range(slabs):
            table = jnp.where(turns == index, float(values[index, 1]), table)
        high = table.astype(BF16)
        depth_t[0, part * square : (part + 1) * square] = high
        depth_t[1, part * square : (part + 1) * square] = (table - high.astype(F32)).astype(BF16)
    loaded(4)
    for part in range(2):
        top = invl_v[part].astype(F32)
        turned = pltpu.roll(top, side, 1)
        left = lax.broadcasted_iota(jnp.int32, top.shape, 1) < side
        invl_t[part, 0:grid] = invl_v[part]
        invl_t[part, grid:] = jnp.where(left, -turned, turned).astype(BF16)
    flipped = jnp.transpose(invl_v[0].astype(F32)).astype(BF16)
    fwdl_t[:, 0:grid] = flipped
    fwdl_t[0:side, grid:] = -flipped[side:]
    fwdl_t[side:, grid:] = flipped[:side]
    loaded(5)
    cosines = jnp.transpose(invr_v[0, 0].astype(F32)).astype(BF16)
    sines = jnp.transpose(invr_v[0, 1].astype(F32)).astype(BF16)
    fwdr_t[0:grid, 0:cells] = cosines
    fwdr_t[0:grid, cells:] = sines
    fwdr_t[grid:, 0:cells] = -sines
    fwdr_t[grid:, cells:] = cosines
    for part in range(2):
        invr_t[part, 0:cells, 0:grid] = invr_v[part, 0]
        invr_t[part, 0:cells, grid:] = -invr_v[part, 1]
        invr_t[part, cells:, 0:grid] = invr_v[part, 1]
        invr_t[part, cells:, grid:] = invr_v[part, 0]

    def depth_dft(image):
        both = jnp.dot(depth_t[0], image, preferred_element_type=F32)
        both = both + jnp.dot(depth_t[1], image, preferred_element_type=F32)
        return both[:cells], turn(both[cells:])

    def coil_images(field):
        field = tidy(field)
        product = s_rr[...] * field + s_ii[...] * swap(field)
        return product.astype(BF16)

    def to_depth(product):
        real, imag = depth_dft(product)
        return (real - imag).astype(BF16).reshape(slabs, halves, padded, width)

    def spectrum(image_ref):
        image = tidy(image_ref[...].astype(F32).reshape(cells, width)).astype(BF16)
        lines = jnp.dot(image, fwdl_t[...], preferred_element_type=F32).astype(BF16)
        stacked = jnp.concatenate([lines[:, :grid], lines[:, grid:]], axis=0)
        return jnp.dot(fwdr_t[...], stacked, preferred_element_type=F32)

    took(trim(b_all.at[0 : coils - 1]), 0)
    product = coil_images(b_all[1 : coils + 1].astype(F32).reshape(cells, width))
    p_send[...] = product.astype(F32).reshape(slabs, halves, padded, width).astype(BF16)
    to_slabs(p_send, p_all, 13, True)
    p_all[j] = p_send[j]
    prior_weights(dims, loaded, cin_v, cmid_v, cout_v, first_w, mid_w, last_w)

    half_here = lax.rem(c, halves)

    @pl.when(j == home)
    def _():
        def share(k):
            other = lax.rem(j + k, slabs)
            remote(b_all.at[1 + halves * other + half_here], b_far, 5, c, other).start()

        repeat(1, slabs, share)
        b_far[...] = b_all[1 + halves * j + half_here]

    @pl.when(mine)
    def _():
        took(k_all.at[0, 0 : across - 1], 2)

    @pl.when(jnp.logical_not(mine))
    def _():
        took(k_all.at[0], 2)

    def pass_on(k):
        other = lax.rem(my_x + k, across)
        remote(k_all.at[:, my_x], k_all.at[:, my_x], 15, other * line + my_y, j).start()

    repeat(1, across, pass_on)

    took(trim(p_all.at[0 : slabs - 1]), 13)
    a_send[...] = to_depth(tidy(p_all[...].astype(F32).reshape(cells, width)).astype(BF16))
    to_slabs(a_send, a_all, 4, True)
    a_all[j] = a_send[j]
    took(trim(s_all.at[0 : slabs - 1]), 1)
    maps = tidy(s_all[...].astype(F32).reshape(cells, width))
    rolled = swap(maps)
    s_rr[...] = jnp.where(low, maps, rolled)
    s_ii[...] = jnp.where(low, -rolled, maps)
    took(trim(a_all.at[0 : slabs - 1]), 4)
    took(k_all.at[:, 0 : across - 1], 15)
    weight = k_all[...].reshape(grid, grid)
    freq = spectrum(a_all)
    kf_keep[0:grid] = weight * freq[:grid]
    kf_keep[grid:] = weight * freq[grid:]
    energy = jnp.sum(kf_keep[...] * freq)

    quarter = lax.broadcasted_iota(jnp.int32, (1, 128), 1) // 32

    def message(values):
        packed = jnp.zeros((1, 128), F32)
        for index, value in enumerate(values):
            packed = jnp.where(quarter == index, value, packed)
        return packed

    third = lax.broadcasted_iota(jnp.int32, (1, width), 1) // (width // 3)

    def as_parts(value):
        value = jnp.broadcast_to(value, (1, width))
        high = value.astype(BF16).astype(F32)
        mid = (value - high).astype(BF16).astype(F32)
        return jnp.where(third == 0, high, jnp.where(third == 1, mid, value - high - mid))

    def with_sums(values, first_sum, second_sum):
        values = jnp.where(row_in_chunk == rows, as_parts(first_sum), values)
        return jnp.where(row_in_chunk == rows + 1, as_parts(second_sum), values)

    def from_parts(line):
        size = width // 3
        joined = line[:, 0:size] + line[:, size : 2 * size] + line[:, 2 * size :]
        return joined[:, 0:1]

    def sum_slabs(src, dst, phase):
        def step(k):
            remote(src, dst.at[j], phase, c, slab_at(k)).start()

        repeat(0, slabs - 1, step)
        dst[j] = src[...]

    scaled = kf_keep[...].astype(BF16)
    back = jnp.dot(invr_t[0], scaled, preferred_element_type=F32)
    back = (back + jnp.dot(invr_t[1], scaled, preferred_element_type=F32)).astype(BF16)
    back = jnp.concatenate([back[:cells], back[cells:]], axis=1)
    image = jnp.dot(back, invl_t[0], preferred_element_type=F32)
    image = (image + jnp.dot(back, invl_t[1], preferred_element_type=F32)) * (1.0 / total)
    bb_part = jnp.sum(right * right)
    image = with_sums(image, energy * (1.0 / total), bb_part)
    c_send[...] = image.astype(BF16).reshape(slabs, halves, padded, width)
    to_slabs(c_send, c_all, 6)
    c_all[j] = c_send[j]
    took(c_all.at[0 : slabs - 1], 6)
    sums = jnp.sum(c_all[:, 0].astype(F32), axis=0)
    energy_sum = from_parts(sums[rows : rows + 1])
    bb_sum = from_parts(sums[rows + 1 : rows + 2])
    image = c_all[...].astype(F32).reshape(cells, width)
    image = jnp.where(row_in_chunk < rows, image, 0.0).astype(BF16)
    real, imag = depth_dft(image)
    image = real + imag
    coil_part = s_rr[...] * image - s_ii[...] * swap(image)
    q_send[...] = with_sums(coil_part, energy_sum, bb_sum).astype(BF16).reshape(coils, padded, width)
    to_coils(lambda other: q_send.at[other], q_all.at[c], 8)
    q_all[c] = q_send[c]

    took(b_near.at[0:2], 16)
    to_planes(b_near, b_halo, 3)

    @pl.when(j != home)
    def _():
        took(b_far, 5)

    chunk_row = lax.broadcasted_iota(jnp.int32, (padded, width), 0)
    b_here = jnp.where(chunk_row < rows, b_far[...].astype(F32), 0.0)
    took(q_all.at[0 : coils - 1], 8)
    sums = jnp.sum(q_all[...].astype(F32), axis=0)
    g_coils = jnp.where(chunk_row < rows, sums, 0.0)
    g_send[...] = g_coils
    g_here = g_coils + REG * b_here
    energy0 = from_parts(sums[rows : rows + 1])
    bb = from_parts(sums[rows + 1 : rows + 2])
    alpha0 = bb / (energy0 + REG * bb)
    resid = b_here - alpha0 * g_here
    r_send[...] = resid.astype(BF16)
    to_coils(lambda other: trim(r_send), trim(r_all.at[c]), 9)
    r_all[c] = r_send[...]

    @pl.when(j == home)
    def _():
        pltpu.make_async_copy(g_send, g_own, recv_sem.at[10]).start()

    @pl.when(j != home)
    def _():
        remote(g_send, g_own, 10, native_coil, native_slab).start()

    rr_part = jnp.sum(resid * resid)
    rb_part = jnp.sum(resid * b_here)

    took(b_halo.at[0:6], 3)
    prior_taps(dims, c, j, b_halo[...], taps, taps_t)
    prior_sums(dims, 0, taps_t, first_w, from_b)

    took(trim(r_all.at[0 : coils - 1]), 9)
    d_send[...] = to_depth(coil_images(r_all[...].astype(F32).reshape(cells, width)))
    to_slabs(d_send, d_all, 11, True)
    d_all[j] = d_send[j]
    took(g_own, 10)
    r_own = b_own[...] - alpha0 * (g_own[...] + REG * b_own[...])
    to_beside(r_own_v, r_near, 17, r_own)
    prior_sums(dims, 1, taps_t, first_w, from_b)
    took(r_near.at[0:2], 17)
    to_planes(r_near, r_halo, 12)

    took(trim(d_all.at[0 : slabs - 1]), 11)
    freq = spectrum(d_all)
    cross = jnp.sum(kf_keep[...] * freq)
    power = freq * freq
    energy = jnp.sum(weight * (power[:grid] + power[grid:]))
    n_send[...] = message([energy * (1.0 / total), cross * (1.0 / total), rr_part, rb_part])
    sum_slabs(n_send, n_all, 7)
    took(r_halo.at[0:6], 12)
    prior_taps(dims, c, j, r_halo[...], taps, taps_t)
    prior_sums(dims, 0, taps_t, first_w, from_r)
    took(n_all.at[0 : slabs - 1], 7)
    n_sum[...] = jnp.sum(n_all[...], axis=0)
    to_coils(lambda other: n_sum, n_tot.at[c], 14)
    n_tot[c] = n_sum[...]
    prior_sums(dims, 1, taps_t, first_w, from_r)

    took(n_tot.at[0 : coils - 1], 14)
    sums = jnp.sum(n_tot[...], axis=0)
    energy1 = sums[:, 0:1]
    cross1 = sums[:, 32:33]
    rr = sums[:, 64:65]
    rb = sums[:, 96:97]
    beta = rr / bb
    curvature = energy1 + 2.0 * beta * cross1 + beta * beta * energy0
    curvature = curvature + REG * (rr + 2.0 * beta * rb + beta * beta * bb)
    alpha1 = rr / curvature
    for_b = alpha0 + alpha1 * beta
    solved = (for_b * b_own[...] + alpha1 * r_own)[0:rows]
    for r in range(rows):
        both_ref[r] = solved[r : r + 1]
    prior_rest(dims, c, j, for_b, alpha1, from_b, from_r, hidden, mid_w, last_w, solved, both_ref.at[pl.ds(rows, rows)])

    @pl.when(j != home)
    def _():
        sent(g_send, 10)

    @pl.when(j == home)
    def _():
        sent(b_all.at[0 : slabs - 1], 5)

    @pl.when(mine)
    def _():
        sent(kern_v.at[0 : slabs - 1], 2)

    sent(trim(b_all.at[0 : coils - 1]), 0)
    sent(trim(s_all.at[0 : slabs - 1]), 1)
    sent(b_halo.at[0:6], 3)
    sent(b_near.at[0:2], 16)
    sent(trim(a_all.at[0 : slabs - 1]), 4)
    sent(c_all.at[0 : slabs - 1], 6)
    sent(n_all.at[0 : slabs - 1], 7)
    sent(q_all.at[0 : coils - 1], 8)
    sent(trim(r_all.at[0 : coils - 1]), 9)
    sent(trim(d_all.at[0 : slabs - 1]), 11)
    sent(r_halo.at[0:6], 12)
    sent(r_near.at[0:2], 17)
    sent(trim(p_all.at[0 : slabs - 1]), 13)
    sent(n_tot.at[0 : coils - 1], 14)
    sent(k_all.at[:, 0 : across - 1], 15)


def prior_weights(dims, loaded, cin_v, cmid_v, cout_v, first_w, mid_w, last_w):
    coils, slabs, halves, rows, padded, side, grid, feats, total = dims
    strip = 3 * padded
    deep = rows + 4
    loaded(6)
    tap_shape = (54, 18 * strip)
    tap = lax.broadcasted_iota(jnp.int32, tap_shape, 0)
    at = lax.broadcasted_iota(jnp.int32, tap_shape, 1)
    kind = at // strip
    place = lax.rem(at, strip)
    inner = lax.rem(place, padded)
    image_row = (place // padded) * rows + inner
    rest = tap - (kind // 6) * 18 - lax.rem(kind, 6)
    for r in range(deep):
        dx = image_row - (r + 3)
        hit = (rest == dx * 6) & (dx >= 0) & (dx < 3) & (inner < rows)
        pick = jnp.where(hit, 1.0, 0.0).astype(BF16)
        part = lax.dot_general(cin_v[...], pick, (((0,), (0,)), ((), ())), preferred_element_type=F32).astype(BF16)
        first_w[2 * r * feats : (2 * r + 1) * feats] = part
        if r > 0:
            first_w[(2 * r - 1) * feats : 2 * r * feats] = part
    first_w[(2 * deep - 1) * feats :] = jnp.zeros((feats, 18 * strip), BF16)
    loaded(7)
    mid_w[...] = jnp.zeros_like(mid_w)
    loaded(8)
    last_w[...] = jnp.zeros_like(last_w)
    for dz in range(3):
        for dx in range(3):
            for dy in range(3):
                first = ((dz * 3 + dx) * 3 + dy) * feats
                block = cmid_v[:, first : first + feats]
                for place in ((0,), (2, 3), (1,))[dy]:
                    mid_w[dz, place * feats : (place + 1) * feats, dx * feats : (dx + 1) * feats] = block
                last_w[dz, dy * 2 : dy * 2 + 2, dx * feats : (dx + 1) * feats] = cout_v[:, first : first + feats]


def shift_lanes(values, up):
    at = lax.broadcasted_iota(jnp.int32, values.shape, 1)
    count = values.shape[1]
    if up:
        return jnp.where(at == 0, 0.0, pltpu.roll(values, 1, 1))
    return jnp.where(at == count - 1, 0.0, pltpu.roll(values, count - 1, 1))


def prior_taps(dims, c, j, field, taps, taps_t):
    coils, slabs, halves, rows, padded, side, grid, feats, total = dims
    strip = 3 * padded
    width = 2 * side
    field = jnp.stack([field[:, k] for k in (0, 2, 1)], axis=1).reshape(21, padded, width)
    index = lax.broadcasted_iota(jnp.int32, (21, padded, width), 0)
    plane = j + index // 3 - 3
    chunk = c + lax.rem(index, 3) - 1
    inside = (plane >= 0) & (plane < slabs) & (chunk >= 0) & (chunk < coils)
    inside = inside & (lax.broadcasted_iota(jnp.int32, (21, padded, width), 1) < rows)
    field = jnp.where(inside, field, 0.0).reshape(7 * strip, width)
    for part in range(2):
        values = field[:, part * side : (part + 1) * side]
        for dy, shifted in enumerate((shift_lanes(values, True), values, shift_lanes(values, False))):
            taps[:, dy * 2 + part] = shifted.reshape(7, strip, side)
    for p in range(5):
        part = jnp.transpose(taps[p : p + 3].reshape(3 * 6 * strip, side))
        high = part.astype(BF16)
        taps_t[0, p] = high
        taps_t[1, p] = (part - high.astype(F32)).astype(BF16)


def prior_sums(dims, turn, taps_t, first_w, result):
    coils, slabs, halves, rows, padded, side, grid, feats, total = dims
    first, last = ((0, 2), (2, 5))[turn]
    inner = 18 * 3 * padded
    contract = (((1,), (1,)), ((), ()))
    tall = (last - first) * side
    high = taps_t[0, first:last].reshape(tall, inner)
    low = taps_t[1, first:last].reshape(tall, inner)
    sums = lax.dot_general(high, first_w[...], contract, preferred_element_type=F32)
    sums = sums + lax.dot_general(low, first_w[...], contract, preferred_element_type=F32)
    result[first:last] = sums.reshape(last - first, side, sums.shape[1])


def prior_rest(dims, c, j, for_b, for_r, from_b, from_r, hidden, mid_w, last_w, solved, out_ref):
    coils, slabs, halves, rows, padded, side, grid, feats, total = dims
    width = 2 * side
    pair = 2 * feats
    deep = rows + 4
    deep_lane = lax.broadcasted_iota(jnp.int32, (1, deep * pair), 1)
    out_row = deep_lane // pair + lax.rem(deep_lane, pair) // feats
    at_row = c * rows - 2 + out_row
    row_ok = (at_row >= 0) & (at_row < side) & (out_row < deep)
    for p in range(5):
        at_plane = j + p - 2
        ok = row_ok & (at_plane >= 0) & (at_plane < slabs)
        scale_b = jnp.where(ok, for_b, 0.0)
        scale_r = jnp.where(ok, for_r, 0.0)
        for r in range(deep):
            span = slice(r * pair, (r + 1) * pair)
            feat = from_b[p, :, span] * scale_b[:, span] + from_r[p, :, span] * scale_r[:, span]
            hidden[p, r] = jnp.maximum(feat, 0.0).astype(BF16)
    wide = rows + 2
    cell = lax.broadcasted_iota(jnp.int32, (side, pair), 0)
    left = lax.broadcasted_iota(jnp.int32, (side, pair), 1) < feats
    result = None
    for p in range(3):
        feat = None
        for dz in range(3):
            data = jnp.concatenate(
                [
                    hidden[p + dz, 0:wide].reshape(wide * side, pair),
                    hidden[p + dz, 2 : wide + 2].reshape(wide * side, pair),
                ],
                axis=1,
            )
            piece = lax.dot_general(data, mid_w[dz], (((1,), (1,)), ((), ())), preferred_element_type=F32)
            feat = piece if feat is None else feat + piece
        at_plane = j + p - 1
        plane_ok = (at_plane >= 0) & (at_plane < slabs)
        maps = []
        for r in range(wide):
            sides = feat[r * side : (r + 1) * side, :pair]
            centre = feat[r * side : (r + 1) * side, pair:]
            ahead = jnp.where(cell == 0, 0.0, pltpu.roll(sides, 1, 0))
            behind = jnp.where(cell == side - 1, 0.0, pltpu.roll(sides, side - 1, 0))
            sides = jnp.where(left, ahead, behind)
            value = jnp.maximum(sides + pltpu.roll(sides, feats, 1) + centre, 0.0)
            at_row = c * rows - 1 + r
            ok = plane_ok & (at_row >= 0) & (at_row < side)
            maps.append(jnp.where(ok, value, 0.0).astype(BF16))
        pairs = [jnp.where(left, maps[r], maps[r + 1]) for r in range(wide - 1)]
        pairs.append(maps[wide - 1])
        data = jnp.concatenate(
            [jnp.concatenate(pairs[0:rows], axis=0), jnp.concatenate(pairs[2 : rows + 2], axis=0)], axis=1
        )
        piece = lax.dot_general(last_w[p], data, (((1,), (1,)), ((), ())), preferred_element_type=F32)
        result = piece if result is None else result + piece
    for r in range(rows):
        span = result[:, r * side : (r + 1) * side]
        value = shift_lanes(span, True)[0:2] + span[2:4] + shift_lanes(span, False)[4:6]
        out_ref[r, :, 0:side] = solved[r : r + 1, 0:side] + value[0:1]
        out_ref[r, :, side:width] = solved[r : r + 1, side:width] + value[1:2]


def shards(adjoint_data, denoised, sensitivity, kernel, conv_in, conv_mid, conv_out):
    coils = lax.axis_size("coil")
    slabs = lax.axis_size("slab")
    rows = adjoint_data.shape[1]
    width = adjoint_data.shape[2]
    side = sensitivity.shape[2]
    grid = kernel.shape[2]
    feats = conv_mid.shape[1]
    halves = coils // slabs
    padded = 8
    deep = rows + 4
    total = float(slabs * grid * grid)
    dims = (coils, slabs, halves, rows, padded, side, grid, feats, total)
    tables = make_tables(slabs, halves, rows, padded, side, grid)
    cells = slabs * halves * padded
    kx = kernel.shape[1]
    layers = (conv_in, conv_mid.T, conv_out.T)
    vmem = pltpu.VMEM
    block = (slabs, halves, padded, width)
    strip = 3 * padded
    scratch = [
        vmem((rows, 1, width), F32), vmem((rows, 1, width), F32), vmem((side, width), F32), vmem((slabs, kx, grid), F32),
        *[vmem(t.shape, BF16) for t in (*tables, *layers)],
        vmem((2, 2 * cells, cells), BF16), vmem((2 * side, 2 * grid), BF16), vmem((2 * grid, 2 * cells), BF16),
        vmem((2, 2 * cells, 2 * grid), BF16), vmem((2, 2 * grid, 2 * side), BF16),
        vmem((padded, width), F32), vmem((padded, width), BF16), vmem((coils + 2, padded, width), BF16),
        vmem((padded, width), BF16), vmem((3, padded, width), F32), vmem((7, 3, padded, width), F32),
        vmem(block, BF16), vmem(block, BF16),
        vmem((slabs // ACROSS, ACROSS, kx, grid), F32),
        vmem((cells, width), F32), vmem((cells, width), F32),
        *[vmem(block, BF16)] * 6,
        vmem((coils, padded, width), BF16), vmem((coils, padded, width), BF16),
        vmem((padded, width), BF16), vmem((coils, padded, width), BF16),
        vmem(block, BF16), vmem(block, BF16),
        vmem((2 * grid, grid), F32),
        vmem((padded, width), F32), vmem((padded, width), F32),
        vmem((padded, width), F32), vmem((3, padded, width), F32), vmem((7, 3, padded, width), F32),
        vmem((1, 128), F32), vmem((1, 128), F32), vmem((slabs, 1, 128), F32), vmem((coils, 1, 128), F32),
        vmem((2 * deep * feats, 18 * strip), BF16), vmem((3, 4 * feats, 4 * feats), BF16), vmem((3, 8, 4 * feats), BF16),
        vmem((7, 6, strip, side), F32), vmem((2, 5, side, 18 * strip), BF16),
        vmem((5, side, 2 * deep * feats), F32), vmem((5, side, 2 * deep * feats), F32),
        vmem((5, deep, side, 2 * feats), BF16),
        pltpu.SemaphoreType.DMA((9,)), pltpu.SemaphoreType.DMA((18,)), pltpu.SemaphoreType.DMA((18,)),
    ]
    near = pl.BlockSpec(memory_space=pltpu.VMEM)
    far = pl.BlockSpec(memory_space=pltpu.HBM)
    shape = jax.ShapeDtypeStruct((2 * rows, 1, width), F32)
    both = pl.pallas_call(
        functools.partial(cg_kernel, dims),
        out_shape=shape,
        in_specs=[far] * 9,
        out_specs=near,
        scratch_shapes=scratch,
        compiler_params=pltpu.CompilerParams(has_side_effects=True, collective_id=0, vmem_limit_bytes=60 << 20),
        name="cg",
    )(adjoint_data.transpose(1, 0, 2), denoised.transpose(1, 0, 2), sensitivity, kernel, *tables, *layers)
    return (both[:rows].transpose(1, 0, 2), both[rows:].transpose(1, 0, 2))


def solution(mesh):
    placed = (
        P("slab", "coil", None),
        P("slab", "coil", None),
        P("coil", "slab", None, None),
        P(None, "slab", None),
        P(),
        P(),
        P(),
    )
    return jax.shard_map(
        shards,
        mesh=mesh,
        in_specs=placed,
        out_specs=(P("slab", "coil", None), P("slab", "coil", None)),
        check_vma=False,
    )
```

```python
import functools

import jax
import jax.numpy as jnp
import numpy as np
from jax import lax
from jax.experimental import pallas as pl
from jax.experimental.pallas import tpu as pltpu
from jax.sharding import PartitionSpec as P

F32 = jnp.float32
BF16 = jnp.bfloat16
REG = 0.5
ACROSS = 4
TRIM = True


def dft_parts(out_len, in_len, length):
    phases = (np.arange(out_len)[:, None] * np.arange(in_len)[None, :] % length) * (2.0 * np.pi / length)
    return np.cos(phases), np.sin(phases)


def in_bf16(table, parts=1):
    rest, out = table, []
    for _ in range(parts):
        part = rest.astype(np.float32).astype(jnp.bfloat16)
        out.append(part)
        rest = rest - part.astype(np.float64)
    return jnp.asarray(np.stack(out))


def make_tables(slabs, halves, rows, padded, side, grid):
    cos_p, sin_p = dft_parts(grid, side, grid)
    cells = slabs * halves * padded
    keep = np.arange(cells) % padded < rows
    cos_x = np.zeros((grid, cells))
    sin_x = np.zeros((grid, cells))
    cos_x[:, keep] = cos_p
    sin_x[:, keep] = sin_p
    return [
        in_bf16(np.stack([cos_x.T, sin_x.T]), 2),
        in_bf16(np.concatenate([cos_p, sin_p], axis=1), 2),
    ]


def cg_kernel(
    dims,
    adj_ref, den_ref, sens_hbm, kern_hbm, invr_hbm, invl_hbm, cin_hbm, cmid_hbm, cout_hbm,
    both_ref,
    adj_v, den_v, sens_v, kern_v, invr_v, invl_v, cin_v, cmid_v, cout_v,
    depth_t, fwdl_t, fwdr_t, invr_t, invl_t,
    b_own, b_send, b_all, b_far, b_near, b_halo, s_send, s_all, k_all, s_rr, s_ii,
    p_send, p_all, a_send, a_all, c_send, c_all, q_send, q_all, r_send, r_all, d_send, d_all, kf_keep,
    g_send, g_own, r_own_v, r_near, r_halo, n_send, n_sum, n_all, n_tot,
    first_w, mid_w, last_w, taps, taps_t, from_b, from_r, hidden,
    load_sem, send_sem, recv_sem,
):
    coils, slabs, halves, rows, padded, side, grid, feats, total = dims
    width = 2 * side
    cells = slabs * padded * halves
    c = lax.axis_index("coil")
    j = lax.axis_index("slab")
    home = c // halves
    across = ACROSS
    line = coils // across
    my_x = c // line
    my_y = lax.rem(c, line)
    lane = lax.broadcasted_iota(jnp.int32, (cells, width), 1)
    low = lane < side
    row_in_chunk = lax.rem(lax.broadcasted_iota(jnp.int32, (cells, width), 0), padded)
    barrier = pltpu.get_barrier_semaphore()
    native_coil = halves * j + lax.rem(c, halves)
    native_slab = c // halves

    def hello(coil, slab):
        pl.semaphore_signal(barrier, inc=1, device_id=to(coil, slab), device_id_type=pl.DeviceIdType.MESH)

    def to(coil, slab):
        return {"coil": coil, "slab": slab}

    def repeat(first, last, body):
        def step(k, carry):
            body(k)
            return carry

        lax.fori_loop(first, last, step, 0)

    def far_first(index, count):
        step = (index + 1) // 2
        return count // 2 + step - 2 * step * lax.rem(index, 2)

    def slab_at(index):
        return lax.rem(j + far_first(index, slabs), slabs)

    def coil_at(index):
        along = lax.rem(my_y + far_first(index // across, line), line)
        return lax.rem(my_x + far_first(lax.rem(index, across), across), across) * line + along

    loads = (
        (adj_ref, adj_v), (den_ref, den_v), (sens_hbm.at[0, 0], sens_v), (kern_hbm, kern_v),
        (invl_hbm, invl_v), (invr_hbm, invr_v), (cin_hbm, cin_v), (cmid_hbm, cmid_v), (cout_hbm, cout_v),
    )
    for index, (src, dst) in enumerate(loads):
        pltpu.make_async_copy(src, dst, load_sem.at[index]).start()

    def loaded(index):
        src, dst = loads[index]
        pltpu.make_async_copy(src, dst, load_sem.at[index]).wait()

    repeat(0, coils - 1, lambda k: hello(coil_at(k), j))
    repeat(0, slabs - 1, lambda k: hello(c, slab_at(k)))

    def trim(ref):
        return ref.at[..., 0:rows, :] if TRIM else ref

    def tidy(values):
        return jnp.where(row_in_chunk < rows, values, 0.0) if TRIM else values

    def swap(values):
        return pltpu.roll(values, side, 1)

    def turn(values):
        rolled = swap(values)
        return jnp.where(low, -rolled, rolled)

    def remote(src, dst, phase, coil, slab):
        return pltpu.make_async_remote_copy(
            src_ref=src,
            dst_ref=dst,
            send_sem=send_sem.at[phase],
            recv_sem=recv_sem.at[phase],
            device_id=to(coil, slab),
            device_id_type=pl.DeviceIdType.MESH,
        )

    def took(ref, phase):
        pltpu.make_async_copy(ref, ref, recv_sem.at[phase]).wait()

    def sent(ref, phase):
        pltpu.make_async_copy(ref, ref, send_sem.at[phase]).wait()

    def to_slabs(src, dst, phase, short=False):
        view = trim if short else lambda ref: ref

        def step(k):
            other = slab_at(k)
            remote(view(src.at[other]), view(dst.at[j]), phase, c, other).start()

        repeat(0, slabs - 1, step)

    def to_coils(pick, dst, phase):
        def step(k):
            other = coil_at(k)
            remote(pick(other), dst, phase, other, j).start()

        repeat(0, coils - 1, step)

    def to_beside(src, dst, phase, values=None):
        if values is not None:
            src[...] = values
        remote(src, dst.at[0], phase, lax.rem(c + 1, coils), j).start()
        remote(src, dst.at[1], phase, lax.rem(c + coils - 1, coils), j).start()
        dst[2] = src[...]

    def to_planes(src, dst, phase):
        def step(k):
            remote(src, dst.at[k], phase, c, lax.rem(j + 3 - k + slabs, slabs)).start()

        repeat(0, 3, step)
        repeat(4, 7, step)
        dst[3] = src[...]

    loaded(0)
    loaded(1)
    right = adj_v[:, 0, :] + REG * den_v[:, 0, :]
    b_own[...] = jnp.zeros_like(b_own)
    b_own[0:rows] = right
    b_send[...] = b_own[...].astype(BF16)
    b_all[0] = jnp.zeros_like(b_send)
    b_all[coils + 1] = jnp.zeros_like(b_send)
    b_all[c + 1] = b_send[...]

    pl.semaphore_wait(barrier, (slabs - 1) + (coils - 1))

    to_coils(lambda other: trim(b_send), trim(b_all.at[c + 1]), 0)
    to_beside(b_own, b_near, 16)

    far_row = j // across
    near_row = lax.rem(j, across)
    mine = near_row == my_x
    loaded(3)

    @pl.when(mine)
    def _():
        def share(k):
            other = lax.rem(j + k, slabs)
            remote(kern_v.at[other], k_all.at[far_row, near_row], 2, c, other).start()

        repeat(1, slabs, share)
        k_all[far_row, near_row] = kern_v[j]

    loaded(2)
    for block in range(slabs):
        for half in range(halves):
            first = (block * halves + half) * rows
            piece = sens_v[first : first + rows, :]
            piece = jnp.concatenate([piece, jnp.zeros((padded - rows, width), F32)], axis=0)
            s_send[block, half] = piece.astype(BF16)
            s_rr[first // rows * padded : (first // rows + 1) * padded] = piece
    to_slabs(s_send, s_all, 1, True)
    s_all[j] = s_send[j]
    maps = s_rr[...]
    rolled = swap(maps)
    s_rr[...] = jnp.where(low, maps, rolled)
    s_ii[...] = jnp.where(low, -rolled, maps)

    square = slabs * halves * padded
    row = lax.broadcasted_iota(jnp.int32, (square, square), 0)
    col = lax.broadcasted_iota(jnp.int32, (square, square), 1)
    group = halves * padded
    turns = lax.rem((row // group) * (col // group), slabs)
    same = (lax.rem(row, group) == lax.rem(col, group)) & (lax.rem(row, padded) < rows)
    turns = jnp.where(same, turns, slabs)
    for part, values in enumerate(dft_parts(slabs, 2, slabs)):
        table = jnp.zeros((square, square), F32)
        for index in range(slabs):
            table = jnp.where(turns == index, float(values[index, 1]), table)
        high = table.astype(BF16)
        depth_t[0, part * square : (part + 1) * square] = high
        depth_t[1, part * square : (part + 1) * square] = (table - high.astype(F32)).astype(BF16)
    loaded(4)
    for part in range(2):
        top = invl_v[part].astype(F32)
        turned = pltpu.roll(top, side, 1)
        left = lax.broadcasted_iota(jnp.int32, top.shape, 1) < side
        invl_t[part, 0:grid] = invl_v[part]
        invl_t[part, grid:] = jnp.where(left, -turned, turned).astype(BF16)
    flipped = jnp.transpose(invl_v[0].astype(F32)).astype(BF16)
    fwdl_t[:, 0:grid] = flipped
    fwdl_t[0:side, grid:] = -flipped[side:]
    fwdl_t[side:, grid:] = flipped[:side]
    loaded(5)
    cosines = jnp.transpose(invr_v[0, 0].astype(F32)).astype(BF16)
    sines = jnp.transpose(invr_v[0, 1].astype(F32)).astype(BF16)
    fwdr_t[0:grid, 0:cells] = cosines
    fwdr_t[0:grid, cells:] = sines
    fwdr_t[grid:, 0:cells] = -sines
    fwdr_t[grid:, cells:] = cosines
    for part in range(2):
        invr_t[part, 0:cells, 0:grid] = invr_v[part, 0]
        invr_t[part, 0:cells, grid:] = -invr_v[part, 1]
        invr_t[part, cells:, 0:grid] = invr_v[part, 1]
        invr_t[part, cells:, grid:] = invr_v[part, 0]

    def depth_dft(image):
        both = jnp.dot(depth_t[0], image, preferred_element_type=F32)
        both = both + jnp.dot(depth_t[1], image, preferred_element_type=F32)
        return both[:cells], turn(both[cells:])

    def coil_images(field):
        field = tidy(field)
        product = s_rr[...] * field + s_ii[...] * swap(field)
        return product.astype(BF16)

    def to_depth(product):
        real, imag = depth_dft(product)
        return (real - imag).astype(BF16).reshape(slabs, halves, padded, width)

    def spectrum(image_ref):
        image = tidy(image_ref[...].astype(F32).reshape(cells, width)).astype(BF16)
        lines = jnp.dot(image, fwdl_t[...], preferred_element_type=F32).astype(BF16)
        stacked = jnp.concatenate([lines[:, :grid], lines[:, grid:]], axis=0)
        return jnp.dot(fwdr_t[...], stacked, preferred_element_type=F32)

    took(trim(b_all.at[0 : coils - 1]), 0)
    product = coil_images(b_all[1 : coils + 1].astype(F32).reshape(cells, width))
    p_send[...] = product.astype(F32).reshape(slabs, halves, padded, width).astype(BF16)
    to_slabs(p_send, p_all, 13, True)
    p_all[j] = p_send[j]
    prior_weights(dims, loaded, cin_v, cmid_v, cout_v, first_w, mid_w, last_w)

    half_here = lax.rem(c, halves)

    @pl.when(j == home)
    def _():
        def share(k):
            other = lax.rem(j + k, slabs)
            remote(b_all.at[1 + halves * other + half_here], b_far, 5, c, other).start()

        repeat(1, slabs, share)
        b_far[...] = b_all[1 + halves * j + half_here]

    @pl.when(mine)
    def _():
        took(k_all.at[0, 0 : across - 1], 2)

    @pl.when(jnp.logical_not(mine))
    def _():
        took(k_all.at[0], 2)

    def pass_on(k):
        other = lax.rem(my_x + k, across)
        remote(k_all.at[:, my_x], k_all.at[:, my_x], 15, other * line + my_y, j).start()

    repeat(1, across, pass_on)

    took(trim(p_all.at[0 : slabs - 1]), 13)
    a_send[...] = to_depth(tidy(p_all[...].astype(F32).reshape(cells, width)).astype(BF16))
    to_slabs(a_send, a_all, 4, True)
    a_all[j] = a_send[j]
    took(trim(s_all.at[0 : slabs - 1]), 1)
    maps = tidy(s_all[...].astype(F32).reshape(cells, width))
    rolled = swap(maps)
    s_rr[...] = jnp.where(low, maps, rolled)
    s_ii[...] = jnp.where(low, -rolled, maps)
    took(trim(a_all.at[0 : slabs - 1]), 4)
    took(k_all.at[:, 0 : across - 1], 15)
    weight = k_all[...].reshape(grid, grid)
    freq = spectrum(a_all)
    kf_keep[0:grid] = weight * freq[:grid]
    kf_keep[grid:] = weight * freq[grid:]
    energy = jnp.sum(kf_keep[...] * freq)

    quarter = lax.broadcasted_iota(jnp.int32, (1, 128), 1) // 32

    def message(values):
        packed = jnp.zeros((1, 128), F32)
        for index, value in enumerate(values):
            packed = jnp.where(quarter == index, value, packed)
        return packed

    third = lax.broadcasted_iota(jnp.int32, (1, width), 1) // (width // 3)

    def as_parts(value):
        value = jnp.broadcast_to(value, (1, width))
        high = value.astype(BF16).astype(F32)
        mid = (value - high).astype(BF16).astype(F32)
        return jnp.where(third == 0, high, jnp.where(third == 1, mid, value - high - mid))

    def with_sums(values, first_sum, second_sum):
        values = jnp.where(row_in_chunk == rows, as_parts(first_sum), values)
        return jnp.where(row_in_chunk == rows + 1, as_parts(second_sum), values)

    def from_parts(line):
        size = width // 3
        joined = line[:, 0:size] + line[:, size : 2 * size] + line[:, 2 * size :]
        return joined[:, 0:1]

    def sum_slabs(src, dst, phase):
        def step(k):
            remote(src, dst.at[j], phase, c, slab_at(k)).start()

        repeat(0, slabs - 1, step)
        dst[j] = src[...]

    scaled = kf_keep[...].astype(BF16)
    back = jnp.dot(invr_t[0], scaled, preferred_element_type=F32)
    back = (back + jnp.dot(invr_t[1], scaled, preferred_element_type=F32)).astype(BF16)
    back = jnp.concatenate([back[:cells], back[cells:]], axis=1)
    image = jnp.dot(back, invl_t[0], preferred_element_type=F32)
    image = (image + jnp.dot(back, invl_t[1], preferred_element_type=F32)) * (1.0 / total)
    bb_part = jnp.sum(right * right)
    image = with_sums(image, energy * (1.0 / total), bb_part)
    c_send[...] = image.astype(BF16).reshape(slabs, halves, padded, width)
    to_slabs(c_send, c_all, 6)
    c_all[j] = c_send[j]
    took(c_all.at[0 : slabs - 1], 6)
    sums = jnp.sum(c_all[:, 0].astype(F32), axis=0)
    energy_sum = from_parts(sums[rows : rows + 1])
    bb_sum = from_parts(sums[rows + 1 : rows + 2])
    image = c_all[...].astype(F32).reshape(cells, width)
    image = jnp.where(row_in_chunk < rows, image, 0.0).astype(BF16)
    real, imag = depth_dft(image)
    image = real + imag
    coil_part = s_rr[...] * image - s_ii[...] * swap(image)
    q_send[...] = with_sums(coil_part, energy_sum, bb_sum).astype(BF16).reshape(coils, padded, width)
    to_coils(lambda other: q_send.at[other], q_all.at[c], 8)
    q_all[c] = q_send[c]

    took(b_near.at[0:2], 16)
    to_planes(b_near, b_halo, 3)

    @pl.when(j != home)
    def _():
        took(b_far, 5)

    chunk_row = lax.broadcasted_iota(jnp.int32, (padded, width), 0)
    b_here = jnp.where(chunk_row < rows, b_far[...].astype(F32), 0.0)
    took(q_all.at[0 : coils - 1], 8)
    sums = jnp.sum(q_all[...].astype(F32), axis=0)
    g_coils = jnp.where(chunk_row < rows, sums, 0.0)
    g_send[...] = g_coils
    g_here = g_coils + REG * b_here
    energy0 = from_parts(sums[rows : rows + 1])
    bb = from_parts(sums[rows + 1 : rows + 2])
    alpha0 = bb / (energy0 + REG * bb)
    resid = b_here - alpha0 * g_here
    r_send[...] = resid.astype(BF16)
    to_coils(lambda other: trim(r_send), trim(r_all.at[c]), 9)
    r_all[c] = r_send[...]

    @pl.when(j == home)
    def _():
        pltpu.make_async_copy(g_send, g_own, recv_sem.at[10]).start()

    @pl.when(j != home)
    def _():
        remote(g_send, g_own, 10, native_coil, native_slab).start()

    rr_part = jnp.sum(resid * resid)
    rb_part = jnp.sum(resid * b_here)

    took(b_halo.at[0:6], 3)
    prior_taps(dims, c, j, b_halo[...], taps, taps_t)
    prior_sums(dims, 0, taps_t, first_w, from_b)

    took(trim(r_all.at[0 : coils - 1]), 9)
    d_send[...] = to_depth(coil_images(r_all[...].astype(F32).reshape(cells, width)))
    to_slabs(d_send, d_all, 11, True)
    d_all[j] = d_send[j]
    took(g_own, 10)
    r_own = b_own[...] - alpha0 * (g_own[...] + REG * b_own[...])
    to_beside(r_own_v, r_near, 17, r_own)
    prior_sums(dims, 1, taps_t, first_w, from_b)
    took(r_near.at[0:2], 17)
    to_planes(r_near, r_halo, 12)

    took(trim(d_all.at[0 : slabs - 1]), 11)
    freq = spectrum(d_all)
    cross = jnp.sum(kf_keep[...] * freq)
    power = freq * freq
    energy = jnp.sum(weight * (power[:grid] + power[grid:]))
    n_send[...] = message([energy * (1.0 / total), cross * (1.0 / total), rr_part, rb_part])
    sum_slabs(n_send, n_all, 7)
    took(n_all.at[0 : slabs - 1], 7)
    n_sum[...] = jnp.sum(n_all[...], axis=0)
    to_coils(lambda other: n_sum, n_tot.at[c], 14)
    n_tot[c] = n_sum[...]
    took(r_halo.at[0:6], 12)
    prior_taps(dims, c, j, r_halo[...], taps, taps_t)
    prior_sums(dims, 0, taps_t, first_w, from_r)
    prior_sums(dims, 1, taps_t, first_w, from_r)

    took(n_tot.at[0 : coils - 1], 14)
    sums = jnp.sum(n_tot[...], axis=0)
    energy1 = sums[:, 0:1]
    cross1 = sums[:, 32:33]
    rr = sums[:, 64:65]
    rb = sums[:, 96:97]
    beta = rr / bb
    curvature = energy1 + 2.0 * beta * cross1 + beta * beta * energy0
    curvature = curvature + REG * (rr + 2.0 * beta * rb + beta * beta * bb)
    alpha1 = rr / curvature
    for_b = alpha0 + alpha1 * beta
    solved = (for_b * b_own[...] + alpha1 * r_own)[0:rows]
    for r in range(rows):
        both_ref[r] = solved[r : r + 1]
    prior_rest(dims, c, j, for_b, alpha1, from_b, from_r, hidden, mid_w, last_w, solved, both_ref.at[pl.ds(rows, rows)])

    @pl.when(j != home)
    def _():
        sent(g_send, 10)

    @pl.when(j == home)
    def _():
        sent(b_all.at[0 : slabs - 1], 5)

    @pl.when(mine)
    def _():
        sent(kern_v.at[0 : slabs - 1], 2)

    sent(trim(b_all.at[0 : coils - 1]), 0)
    sent(trim(s_all.at[0 : slabs - 1]), 1)
    sent(b_halo.at[0:6], 3)
    sent(b_near.at[0:2], 16)
    sent(trim(a_all.at[0 : slabs - 1]), 4)
    sent(c_all.at[0 : slabs - 1], 6)
    sent(n_all.at[0 : slabs - 1], 7)
    sent(q_all.at[0 : coils - 1], 8)
    sent(trim(r_all.at[0 : coils - 1]), 9)
    sent(trim(d_all.at[0 : slabs - 1]), 11)
    sent(r_halo.at[0:6], 12)
    sent(r_near.at[0:2], 17)
    sent(trim(p_all.at[0 : slabs - 1]), 13)
    sent(n_tot.at[0 : coils - 1], 14)
    sent(k_all.at[:, 0 : across - 1], 15)


def prior_weights(dims, loaded, cin_v, cmid_v, cout_v, first_w, mid_w, last_w):
    coils, slabs, halves, rows, padded, side, grid, feats, total = dims
    strip = 3 * padded
    deep = rows + 4
    loaded(6)
    tap_shape = (54, 18 * strip)
    tap = lax.broadcasted_iota(jnp.int32, tap_shape, 0)
    at = lax.broadcasted_iota(jnp.int32, tap_shape, 1)
    kind = at // strip
    place = lax.rem(at, strip)
    inner = lax.rem(place, padded)
    image_row = (place // padded) * rows + inner
    rest = tap - (kind // 6) * 18 - lax.rem(kind, 6)
    for r in range(deep):
        dx = image_row - (r + 3)
        hit = (rest == dx * 6) & (dx >= 0) & (dx < 3) & (inner < rows)
        pick = jnp.where(hit, 1.0, 0.0).astype(BF16)
        part = lax.dot_general(cin_v[...], pick, (((0,), (0,)), ((), ())), preferred_element_type=F32).astype(BF16)
        first_w[2 * r * feats : (2 * r + 1) * feats] = part
        if r > 0:
            first_w[(2 * r - 1) * feats : 2 * r * feats] = part
    first_w[(2 * deep - 1) * feats :] = jnp.zeros((feats, 18 * strip), BF16)
    loaded(7)
    mid_w[...] = jnp.zeros_like(mid_w)
    loaded(8)
    last_w[...] = jnp.zeros_like(last_w)
    for dz in range(3):
        for dx in range(3):
            for dy in range(3):
                first = ((dz * 3 + dx) * 3 + dy) * feats
                block = cmid_v[:, first : first + feats]
                for place in ((0,), (2, 3), (1,))[dy]:
                    mid_w[dz, place * feats : (place + 1) * feats, dx * feats : (dx + 1) * feats] = block
                last_w[dz, dy * 2 : dy * 2 + 2, dx * feats : (dx + 1) * feats] = cout_v[:, first : first + feats]


def shift_lanes(values, up):
    at = lax.broadcasted_iota(jnp.int32, values.shape, 1)
    count = values.shape[1]
    if up:
        return jnp.where(at == 0, 0.0, pltpu.roll(values, 1, 1))
    return jnp.where(at == count - 1, 0.0, pltpu.roll(values, count - 1, 1))


def prior_taps(dims, c, j, field, taps, taps_t):
    coils, slabs, halves, rows, padded, side, grid, feats, total = dims
    strip = 3 * padded
    width = 2 * side
    field = jnp.stack([field[:, k] for k in (0, 2, 1)], axis=1).reshape(21, padded, width)
    index = lax.broadcasted_iota(jnp.int32, (21, padded, width), 0)
    plane = j + index // 3 - 3
    chunk = c + lax.rem(index, 3) - 1
    inside = (plane >= 0) & (plane < slabs) & (chunk >= 0) & (chunk < coils)
    inside = inside & (lax.broadcasted_iota(jnp.int32, (21, padded, width), 1) < rows)
    field = jnp.where(inside, field, 0.0).reshape(7 * strip, width)
    for part in range(2):
        values = field[:, part * side : (part + 1) * side]
        for dy, shifted in enumerate((shift_lanes(values, True), values, shift_lanes(values, False))):
            taps[:, dy * 2 + part] = shifted.reshape(7, strip, side)
    for p in range(5):
        part = jnp.transpose(taps[p : p + 3].reshape(3 * 6 * strip, side))
        high = part.astype(BF16)
        taps_t[0, p] = high
        taps_t[1, p] = (part - high.astype(F32)).astype(BF16)


def prior_sums(dims, turn, taps_t, first_w, result):
    coils, slabs, halves, rows, padded, side, grid, feats, total = dims
    first, last = ((0, 2), (2, 5))[turn]
    inner = 18 * 3 * padded
    contract = (((1,), (1,)), ((), ()))
    tall = (last - first) * side
    high = taps_t[0, first:last].reshape(tall, inner)
    low = taps_t[1, first:last].reshape(tall, inner)
    sums = lax.dot_general(high, first_w[...], contract, preferred_element_type=F32)
    sums = sums + lax.dot_general(low, first_w[...], contract, preferred_element_type=F32)
    result[first:last] = sums.reshape(last - first, side, sums.shape[1])


def prior_rest(dims, c, j, for_b, for_r, from_b, from_r, hidden, mid_w, last_w, solved, out_ref):
    coils, slabs, halves, rows, padded, side, grid, feats, total = dims
    width = 2 * side
    pair = 2 * feats
    deep = rows + 4
    deep_lane = lax.broadcasted_iota(jnp.int32, (1, deep * pair), 1)
    out_row = deep_lane // pair + lax.rem(deep_lane, pair) // feats
    at_row = c * rows - 2 + out_row
    row_ok = (at_row >= 0) & (at_row < side) & (out_row < deep)
    for p in range(5):
        at_plane = j + p - 2
        ok = row_ok & (at_plane >= 0) & (at_plane < slabs)
        scale_b = jnp.where(ok, for_b, 0.0)
        scale_r = jnp.where(ok, for_r, 0.0)
        for r in range(deep):
            span = slice(r * pair, (r + 1) * pair)
            feat = from_b[p, :, span] * scale_b[:, span] + from_r[p, :, span] * scale_r[:, span]
            hidden[p, r] = jnp.maximum(feat, 0.0).astype(BF16)
    wide = rows + 2
    cell = lax.broadcasted_iota(jnp.int32, (side, pair), 0)
    left = lax.broadcasted_iota(jnp.int32, (side, pair), 1) < feats
    result = None
    for p in range(3):
        feat = None
        for dz in range(3):
            data = jnp.concatenate(
                [
                    hidden[p + dz, 0:wide].reshape(wide * side, pair),
                    hidden[p + dz, 2 : wide + 2].reshape(wide * side, pair),
                ],
                axis=1,
            )
            piece = lax.dot_general(data, mid_w[dz], (((1,), (1,)), ((), ())), preferred_element_type=F32)
            feat = piece if feat is None else feat + piece
        at_plane = j + p - 1
        plane_ok = (at_plane >= 0) & (at_plane < slabs)
        maps = []
        for r in range(wide):
            sides = feat[r * side : (r + 1) * side, :pair]
            centre = feat[r * side : (r + 1) * side, pair:]
            ahead = jnp.where(cell == 0, 0.0, pltpu.roll(sides, 1, 0))
            behind = jnp.where(cell == side - 1, 0.0, pltpu.roll(sides, side - 1, 0))
            sides = jnp.where(left, ahead, behind)
            value = jnp.maximum(sides + pltpu.roll(sides, feats, 1) + centre, 0.0)
            at_row = c * rows - 1 + r
            ok = plane_ok & (at_row >= 0) & (at_row < side)
            maps.append(jnp.where(ok, value, 0.0).astype(BF16))
        pairs = [jnp.where(left, maps[r], maps[r + 1]) for r in range(wide - 1)]
        pairs.append(maps[wide - 1])
        data = jnp.concatenate(
            [jnp.concatenate(pairs[0:rows], axis=0), jnp.concatenate(pairs[2 : rows + 2], axis=0)], axis=1
        )
        piece = lax.dot_general(last_w[p], data, (((1,), (1,)), ((), ())), preferred_element_type=F32)
        result = piece if result is None else result + piece
    for r in range(rows):
        span = result[:, r * side : (r + 1) * side]
        value = shift_lanes(span, True)[0:2] + span[2:4] + shift_lanes(span, False)[4:6]
        out_ref[r, :, 0:side] = solved[r : r + 1, 0:side] + value[0:1]
        out_ref[r, :, side:width] = solved[r : r + 1, side:width] + value[1:2]


def shards(adjoint_data, denoised, sensitivity, kernel, conv_in, conv_mid, conv_out):
    coils = lax.axis_size("coil")
    slabs = lax.axis_size("slab")
    rows = adjoint_data.shape[1]
    width = adjoint_data.shape[2]
    side = sensitivity.shape[2]
    grid = kernel.shape[2]
    feats = conv_mid.shape[1]
    halves = coils // slabs
    padded = 8
    deep = rows + 4
    total = float(slabs * grid * grid)
    dims = (coils, slabs, halves, rows, padded, side, grid, feats, total)
    tables = make_tables(slabs, halves, rows, padded, side, grid)
    cells = slabs * halves * padded
    kx = kernel.shape[1]
    layers = (conv_in, conv_mid.T, conv_out.T)
    vmem = pltpu.VMEM
    block = (slabs, halves, padded, width)
    strip = 3 * padded
    scratch = [
        vmem((rows, 1, width), F32), vmem((rows, 1, width), F32), vmem((side, width), F32), vmem((slabs, kx, grid), F32),
        *[vmem(t.shape, BF16) for t in (*tables, *layers)],
        vmem((2, 2 * cells, cells), BF16), vmem((2 * side, 2 * grid), BF16), vmem((2 * grid, 2 * cells), BF16),
        vmem((2, 2 * cells, 2 * grid), BF16), vmem((2, 2 * grid, 2 * side), BF16),
        vmem((padded, width), F32), vmem((padded, width), BF16), vmem((coils + 2, padded, width), BF16),
        vmem((padded, width), BF16), vmem((3, padded, width), F32), vmem((7, 3, padded, width), F32),
        vmem(block, BF16), vmem(block, BF16),
        vmem((slabs // ACROSS, ACROSS, kx, grid), F32),
        vmem((cells, width), F32), vmem((cells, width), F32),
        *[vmem(block, BF16)] * 6,
        vmem((coils, padded, width), BF16), vmem((coils, padded, width), BF16),
        vmem((padded, width), BF16), vmem((coils, padded, width), BF16),
        vmem(block, BF16), vmem(block, BF16),
        vmem((2 * grid, grid), F32),
        vmem((padded, width), F32), vmem((padded, width), F32),
        vmem((padded, width), F32), vmem((3, padded, width), F32), vmem((7, 3, padded, width), F32),
        vmem((1, 128), F32), vmem((1, 128), F32), vmem((slabs, 1, 128), F32), vmem((coils, 1, 128), F32),
        vmem((2 * deep * feats, 18 * strip), BF16), vmem((3, 4 * feats, 4 * feats), BF16), vmem((3, 8, 4 * feats), BF16),
        vmem((7, 6, strip, side), F32), vmem((2, 5, side, 18 * strip), BF16),
        vmem((5, side, 2 * deep * feats), F32), vmem((5, side, 2 * deep * feats), F32),
        vmem((5, deep, side, 2 * feats), BF16),
        pltpu.SemaphoreType.DMA((9,)), pltpu.SemaphoreType.DMA((18,)), pltpu.SemaphoreType.DMA((18,)),
    ]
    near = pl.BlockSpec(memory_space=pltpu.VMEM)
    far = pl.BlockSpec(memory_space=pltpu.HBM)
    shape = jax.ShapeDtypeStruct((2 * rows, 1, width), F32)
    both = pl.pallas_call(
        functools.partial(cg_kernel, dims),
        out_shape=shape,
        in_specs=[far] * 9,
        out_specs=near,
        scratch_shapes=scratch,
        compiler_params=pltpu.CompilerParams(has_side_effects=True, collective_id=0, vmem_limit_bytes=60 << 20),
        name="cg",
    )(adjoint_data.transpose(1, 0, 2), denoised.transpose(1, 0, 2), sensitivity, kernel, *tables, *layers)
    return (both[:rows].transpose(1, 0, 2), both[rows:].transpose(1, 0, 2))


def solution(mesh):
    placed = (
        P("slab", "coil", None),
        P("slab", "coil", None),
        P("coil", "slab", None, None),
        P(None, "slab", None),
        P(),
        P(),
        P(),
    )
    return jax.shard_map(
        shards,
        mesh=mesh,
        in_specs=placed,
        out_specs=(P("slab", "coil", None), P("slab", "coil", None)),
        check_vma=False,
    )
```
